32 devices in a mesh: stream: 2 (over x), dp: 16 (over z, y, core).
Axes of the slice: x: 2, y: 2, z: 4, core: 2. Of those that a mesh axis runs over, the one named last changes fastest.
Arguments:
- tokens: bfloat16 [2, 16, 512, 768], P('stream', 'dp'), may hold values from -6 to 6
- boxes: int32 [2, 16, 2, 512], P('stream', 'dp'), may hold values from 0 to 1023
- rel_one: int32 [2, 16, 512, 512], P('stream', 'dp'), may hold values from 0 to 31
- rel_two: int32 [2, 16, 512, 512], P('stream', 'dp'), may hold values from 0 to 63
- vis_count: int32 [16], P('dp'), may hold values from 256 to 512, as said below
- spatial_tables: bfloat16 [2, 1024, 768], replicated, may hold values from -4.1875 to 4.1875
- proj_weights: bfloat16 [2, 2, 5, 768, 768], P('stream'), may hold values from -0.21875 to 0.21875
- out_weights: bfloat16 [2, 2, 768, 768], P('stream'), may hold values from -1.25 to 1.25
- ffn_in: bfloat16 [2, 2, 768, 3072], P('stream'), may hold values from -0.21875 to 0.21875
- ffn_out: bfloat16 [2, 2, 3072, 768], P('stream'), may hold values from -0.109375 to 0.109375
- norm_gains: float32 [2, 2, 2, 768], P('stream'), may hold values from 0.5 to 1.5
- norm_shifts: float32 [2, 2, 2, 768], P('stream'), may hold values from -1.8 to 1.8
- bias_tables: bfloat16 [2, 2, 12, 96], P('stream'), may hold values from -6 to 6
- cotangent: bfloat16 [2, 16, 512, 768], P('stream', 'dp'), may hold values from -6 to 6
Outputs:
- output: bfloat16 [2, 16, 512, 768], P('stream', 'dp')
- grad_tokens: float32 [2, 16, 512, 768], P('stream', 'dp')
- grad_spatial: float32 [2, 1024, 768], replicated
- grad_proj: float32 [2, 2, 5, 768, 768], P('stream', None, None, 'dp')
- grad_out: float32 [2, 2, 768, 768], P('stream', None, 'dp')
- grad_ffn_in: float32 [2, 2, 768, 3072], P('stream', None, 'dp')
- grad_ffn_out: float32 [2, 2, 3072, 768], P('stream', None, 'dp')
- grad_gains: float32 [2, 2, 2, 768], P('stream', None, None, 'dp')
- grad_shifts: float32 [2, 2, 2, 768], P('stream', None, None, 'dp')
- grad_tables: float32 [2, 2, 12, 96], P('stream')
The draws below stay inside these ranges and needn't reach their ends.
Inputs may be any that keep to these rules, and one draw needn't show every extreme that they name: `vis_count`: each page has 256 or 512 visual tokens; the first page always has 512, the second 512 // 2.
All inputs are finite; a program needn't handle non-finite values.
Results may differ from the reference program's by a relative error of at most 0.035.
The reference program's roundings to bfloat16 on the way count: a program that leaves them out, or rounds other values in their place, can miss the bound.
Values sent between devices are 32-bit elements; how exact they have to be, the bound alone decides.
No kernel may reach another device: no remote copies, remote signals or barrier semaphores. Data moves between devices by JAX's collectives and lax.ppermute only.
A program may use at most 384 MiB of HBM per device.

```python
import jax
import jax.numpy as jnp
from jax import lax

D = 768
HEADS = 12
HD = 64
FF = 3072
SEQ = 512
BINS = 1024
NB1 = 32
NB2 = 64
LAYERS = 2
NBT = 96
PAGES = 16


def draw_vis_count(key, part):
    choose = jax.random.randint(key, (PAGES,), 0, 2)
    places = jnp.arange(PAGES)
    choose = jnp.where(places == 0, 1, jnp.where(places == 1, 0, choose))
    return (SEQ // 2 + SEQ // 2 * choose).astype(jnp.int32)


def plant(values, stream_key, least, high):
    place = [jax.random.randint(jax.random.fold_in(stream_key, axis), (), 0, length) for axis, length in enumerate(values.shape)]
    widest = values.shape.index(max(values.shape))
    next_to = place[:widest] + [(place[widest] + 1) % values.shape[widest]] + place[widest + 1:]
    return values.at[tuple(place)].set(least).at[tuple(next_to)].set(high)


def block_levels(rng, shape, split, least, top_value):
    def one(position, shards_of):
        heights = jax.random.uniform(jax.random.fold_in(jax.random.fold_in(rng, 6), position), (shards_of,), jnp.float32, least / len(split), top_value / len(split))
        return jnp.repeat(jnp.exp(heights), shape[position] // shards_of).reshape((-1,) + (1,) * (len(shape) - position - 1))

    gain = one(*split[0])
    for cut in split[1:]:
        gain = gain * one(*cut)
    return gain


def noise(rng, extent, width, limit, split=(), kind=jnp.bfloat16):
    array = width * jax.random.normal(rng, extent, jnp.float32)
    if split:
        array = array * block_levels(rng, extent, split, -0.22, 0.18)
    return jnp.clip(array, -limit, limit).astype(kind)


def setup_inputs(seed: int = 0) -> dict:
    seeds = jax.random.split(jax.random.key(seed), 15)
    return {
        "tokens": noise(seeds[0], (2, PAGES, SEQ, D), 1.0, 6.0, ((0, 2), (1, 16))),
        "boxes": plant(jax.random.randint(seeds[1], (2, PAGES, 2, SEQ), 0, BINS), jax.random.fold_in(seeds[1], 1), 0, BINS - 1).astype(jnp.int32),
        "rel_one": plant(jax.random.randint(seeds[2], (2, PAGES, SEQ, SEQ), 0, NB1), jax.random.fold_in(seeds[2], 1), 0, NB1 - 1).astype(jnp.int32),
        "rel_two": plant(jax.random.randint(seeds[3], (2, PAGES, SEQ, SEQ), 0, NB2), jax.random.fold_in(seeds[3], 1), 0, NB2 - 1).astype(jnp.int32),
        "vis_count": draw_vis_count(jax.random.fold_in(seeds[14], 71), 0),
        "spatial_tables": noise(seeds[5], (2, BINS, D), 0.7, 4.1875),
        "proj_weights": noise(seeds[6], (2, LAYERS, 5, D, D), D ** -0.5, 0.21875, ((0, 2),)),
        "out_weights": noise(seeds[7], (2, LAYERS, D, D), (D // 32) ** -0.5, 1.25, ((0, 2),)),
        "ffn_in": noise(seeds[8], (2, LAYERS, D, FF), D ** -0.5, 0.21875, ((0, 2),)),
        "ffn_out": noise(seeds[9], (2, LAYERS, FF, D), FF ** -0.5, 0.109375, ((0, 2),)),
        "norm_gains": jnp.clip(1.0 + 0.1 * jax.random.normal(seeds[10], (2, LAYERS, 2, D), jnp.float32), 0.5, 1.5),
        "norm_shifts": noise(seeds[11], (2, LAYERS, 2, D), 0.3, 1.8, ((0, 2),), jnp.float32),
        "bias_tables": noise(seeds[12], (2, LAYERS, HEADS, NBT), 1.0, 6.0, ((0, 2),)),
        "cotangent": noise(seeds[13], (2, PAGES, SEQ, D), 1.0, 6.0, ((0, 2), (1, 16))),
    }


@jax.custom_vjp
def low(v):
    return lax.optimization_barrier(v.astype(jnp.bfloat16)).astype(jnp.float32)

@jax.custom_vjp
def low_back(v):
    return v

def low_keep(v):
    return (low(v), None)

def low_pass(kept, grad):
    return (grad,)

def back_keep(v):
    return (v, None)

def back_low(kept, grad):
    return (low(grad),)
low.defvjp(low_keep, low_pass)
low_back.defvjp(back_keep, back_low)
NEG_FILL = -1e+30

def layer_norm(values, gain_vec, shift_vec):
    center = values - lax.optimization_barrier(jnp.mean(values, axis=-1, keepdims=True))
    spread = lax.optimization_barrier(jnp.mean(center * center, axis=-1, keepdims=True))
    return center * lax.rsqrt(spread + 1e-05) * gain_vec + shift_vec

def matmul(left, right):
    return jnp.dot(left, right, precision=lax.Precision.HIGHEST)

def split_heads(values):
    return values.reshape(values.shape[0], HEADS, HD)

def attend(hidden_in, spatial, projections, out_proj, bucket_table, rel_first, rel_second, key_count):
    rounded = low(hidden_in)
    queries = low(low_back(matmul(rounded, projections[0])))
    keys_all = low(low_back(matmul(rounded, projections[1])))
    values_all = low(low_back(matmul(rounded, projections[2])))
    spatial_q = low(low_back(matmul(spatial, projections[3])))
    spatial_k = low(low_back(matmul(spatial, projections[4])))
    query_cat = jnp.concatenate([split_heads(queries), split_heads(spatial_q)], axis=-1)
    key_cat = jnp.concatenate([split_heads(keys_all), split_heads(spatial_k)], axis=-1)
    scores = jnp.einsum('qhd,khd->hqk', query_cat, key_cat, precision=lax.Precision.HIGHEST) * HD ** (-0.5)
    scores = scores + jnp.take(bucket_table, rel_first, axis=1) + jnp.take(bucket_table, rel_second + NB1, axis=1)
    scores = low_back(scores)
    positions = jnp.arange(SEQ)
    key_valid = positions < key_count
    scores = jnp.where(key_valid[None, None, :], scores, NEG_FILL)
    prob_low = low(jax.nn.softmax(scores, axis=-1))
    context = jnp.einsum('hqk,khd->qhd', prob_low, split_heads(values_all), precision=lax.Precision.HIGHEST)
    context = low(low_back(context.reshape(SEQ, D)))
    rowmask = key_valid.astype(jnp.float32)[:, None]
    return low_back(matmul(context, out_proj)) * rowmask

def page_forward(tokens_page, spatial_tables, proj_weights, out_weights, ffn_in, ffn_out, norm_gains, norm_shifts, bias_tables, boxes_page, rel_one_page, rel_two_page, key_count):
    counts = (SEQ, key_count)
    streams = []
    spatials = []
    for stream_at in range(2):
        spatial_sum = jnp.take(spatial_tables[0], boxes_page[stream_at, 0], axis=0) + jnp.take(spatial_tables[1], boxes_page[stream_at, 1], axis=0)
        spatials.append(low(low_back(spatial_sum)))
        streams.append(tokens_page[stream_at])
    for layer_at in range(LAYERS):
        branches = []
        for stream_at in range(2):
            branches.append(attend(streams[stream_at], spatials[stream_at], proj_weights[stream_at, layer_at], out_weights[stream_at, layer_at], bias_tables[stream_at, layer_at], rel_one_page[stream_at], rel_two_page[stream_at], counts[stream_at]))
        mixed = branches[0] + branches[1]
        for stream_at in range(2):
            normed = layer_norm(streams[stream_at] + mixed, norm_gains[stream_at, layer_at, 0], norm_shifts[stream_at, layer_at, 0])
            inner_pre = low_back(matmul(low(normed), ffn_in[stream_at, layer_at]))
            activated = low(jax.nn.gelu(inner_pre, approximate=False))
            branch = low_back(matmul(activated, ffn_out[stream_at, layer_at]))
            streams[stream_at] = layer_norm(normed + branch, norm_gains[stream_at, layer_at, 1], norm_shifts[stream_at, layer_at, 1])
    rowmask = (jnp.arange(SEQ) < key_count).astype(jnp.float32)[:, None]
    return jnp.stack([streams[0], streams[1] * rowmask])

def reference(tokens, boxes, rel_one, rel_two, vis_count, spatial_tables, proj_weights, out_weights, ffn_in, ffn_out, norm_gains, norm_shifts, bias_tables, cotangent):
    params = tuple((weight_arr.astype(jnp.float32) for weight_arr in (spatial_tables, proj_weights, out_weights, ffn_in, ffn_out, norm_gains, norm_shifts, bias_tables)))

    def one_page(totals, page_data):
        tokens_page, boxes_page, first_page, second_page, key_count, cot_page = page_data

        def forward(tokens_in, *weights):
            return page_forward(tokens_in, *weights, boxes_page, first_page, second_page, key_count)
        result, pullback = jax.vjp(forward, tokens_page.astype(jnp.float32), *params)
        gradients = pullback(cot_page.astype(jnp.float32))
        totals = tuple((summed + gradient for summed, gradient in zip(totals, gradients[1:])))
        return (totals, (result.astype(jnp.bfloat16), gradients[0]))
    page_slices = (jnp.swapaxes(tokens, 0, 1), jnp.swapaxes(boxes, 0, 1), jnp.swapaxes(rel_one, 0, 1), jnp.swapaxes(rel_two, 0, 1), vis_count, jnp.swapaxes(cotangent, 0, 1))
    zero_sums = tuple((jnp.zeros(weight_arr.shape, jnp.float32) for weight_arr in params))
    totals, (results, token_grads) = lax.scan(one_page, zero_sums, page_slices)
    return (jnp.swapaxes(results, 0, 1), jnp.swapaxes(token_grads, 0, 1), totals[0], totals[1], totals[2], totals[3], totals[4], totals[5], totals[6], totals[7])
```

```python
from functools import partial

import jax
import jax.numpy as jnp
from jax import lax
from jax.experimental import pallas as pl
from jax.experimental.pallas import tpu as pltpu
from jax.sharding import PartitionSpec as P

D = 768
HEADS = 12
HD = 64
NB1 = 32
NB2 = 64
LAYERS = 2
LANES = 128
NEG_FILL = -1e30
EPS = 1e-05
SCALE = HD ** (-0.5)
SQRT_HALF = 0.5**0.5
DENSITY = 0.3989422804014327
SWAP = [(0, 1), (1, 0)]
VMEM_LIMIT = 48 << 20
COST = pl.CostEstimate(flops=10**13, bytes_accessed=10**9, transcendentals=0)


def dot(left, right, left_dim=1, right_dim=0):
    return lax.dot_general(
        left, right, (((left_dim,), (right_dim,)), ((), ())), preferred_element_type=jnp.float32
    )


def low(values):
    return values.astype(jnp.bfloat16)


def gate(values, *deps):
    return lax.optimization_barrier((values,) + deps)[0]


class Order:
    def __init__(self):
        self.last = ()

    def call(self, kernel, shapes, operands, in_specs, out_specs, grid, name, scratch=(), scalars=()):
        after = tuple(self.last)
        taken = len(scalars) + len(operands)

        def body(*refs):
            kernel(*refs[:taken], *refs[taken + len(after) :])

        single = not isinstance(shapes, list)
        results = pl.pallas_call(
            body,
            grid_spec=pltpu.PrefetchScalarGridSpec(
                num_scalar_prefetch=len(scalars),
                grid=grid,
                in_specs=list(in_specs) + [pl.BlockSpec(memory_space=pl.ANY)] * len(after),
                out_specs=out_specs,
                scratch_shapes=list(scratch),
            ),
            out_shape=shapes,
            compiler_params=pltpu.CompilerParams(vmem_limit_bytes=VMEM_LIMIT),
            cost_estimate=COST,
            name=name,
        )(*scalars, *operands, *after)
        self.last = (results if single else results[0],)
        return results


def whole_spec(shape):
    return pl.BlockSpec(shape, lambda *ids: (0,) * len(shape))


def bias_kernel(one_ref, two_ref, table_ref, bias_ref):
    rows, length = one_ref.shape

    def group(step, carry):
        span = pl.ds(pl.multiple_of(step * 8, 8), 8)
        for col in range(0, length, LANES):
            cols = slice(col, col + LANES)
            first = one_ref[span, cols]
            second = two_ref[span, cols]
            for head in range(HEADS):
                first_row = jnp.broadcast_to(table_ref[0, head : head + 1, :], (8, LANES))
                second_row = jnp.broadcast_to(table_ref[1, head : head + 1, :], (8, LANES))
                bias_ref[head, span, cols] = jnp.take_along_axis(
                    first_row, first, axis=1
                ) + jnp.take_along_axis(second_row, second, axis=1)
        return carry

    lax.fori_loop(0, rows // 8, group, 0)


def score_bias(rel_one, rel_two, table, at, rows):
    length = rel_one.shape[1]
    step = 64
    first = at * rows // step
    rel = pl.BlockSpec((step, length), lambda i: (first + i, 0))
    return pl.pallas_call(
        bias_kernel,
        grid=(rows // step,),
        in_specs=[rel, rel, whole_spec(table.shape)],
        out_specs=pl.BlockSpec((HEADS, step, length), lambda i: (0, i, 0)),
        out_shape=jax.ShapeDtypeStruct((HEADS, rows, length), jnp.float32),
        cost_estimate=COST,
        name="score_bias",
    )(rel_one, rel_two, table)


def attend_kernel(
    at,
    tile,
    count_ref,
    query_ref,
    key_ref,
    value_ref,
    squery_ref,
    skey_ref,
    bias_ref,
    out_w_ref,
    context_ref,
    attn_ref,
    prob_ref,
    score_ref,
    low_ref,
):
    pair = pl.program_id(0)
    rows = query_ref.shape[0]
    length = value_ref.shape[0]
    lanes = lax.broadcasted_iota(jnp.int32, (1, 2 * HD), 1)
    valid = lax.broadcasted_iota(jnp.int32, (1, length), 1) < count_ref[0]
    keys = jnp.concatenate([key_ref[...], skey_ref[...]], axis=0)
    for half in range(2):
        keep = low(((lanes >= HD) == (half == 1)).astype(jnp.float32) * SCALE)
        queries = jnp.concatenate([query_ref[...] * keep, squery_ref[...] * keep], axis=1)
        score_ref[half] = dot(queries, keys)

    def group(step, carry):
        span = pl.ds(pl.multiple_of(step * tile, tile), tile)
        for half in range(2):
            scores = score_ref[half, span, :] + bias_ref[half, span, :]
            scores = jnp.where(valid, scores, NEG_FILL)
            weights = jnp.exp(scores - jnp.max(scores, axis=1, keepdims=True))
            prob = weights * (1.0 / jnp.sum(weights, axis=1, keepdims=True))
            prob_ref[half, span, :] = prob
            low_ref[half, span, :] = low(prob)
        return carry

    lax.fori_loop(0, rows // tile, group, 0)
    first = dot(low_ref[0], value_ref[...])
    second = dot(low_ref[1], value_ref[...])
    cols = pl.ds(pl.multiple_of(pair * 2 * HD, 2 * HD), 2 * HD)
    context_ref[:, cols] = low(jnp.where(lanes >= HD, second, first))

    @pl.when(pair == pl.num_programs(0) - 1)
    def finish():
        index = lax.broadcasted_iota(jnp.int32, (rows, 1), 0) + at * rows
        mask = (index < count_ref[0]).astype(jnp.float32)
        attn_ref[...] = dot(context_ref[...], out_w_ref[...]) * mask


def attend(count, projected, bias, out_w, layer_at, at, rows):
    query, key_t, value, squery, skey_t = projected
    length = value.shape[0]
    row_pair = pl.BlockSpec((rows, 2 * HD), lambda p, c: (at, p))
    key_pair = pl.BlockSpec((2 * HD, length), lambda p, c: (p, 0))
    value_pair = pl.BlockSpec((length, 2 * HD), lambda p, c: (0, p))
    score_pair = pl.BlockSpec((2, rows, length), lambda p, c: (p, 0, 0))
    return pl.pallas_call(
        partial(attend_kernel, at, 128),
        grid_spec=pltpu.PrefetchScalarGridSpec(
            num_scalar_prefetch=1,
            grid=(HEADS // 2,),
            in_specs=[
                row_pair,
                key_pair,
                value_pair,
                row_pair,
                key_pair,
                score_pair,
                pl.BlockSpec((None, None, D, D), lambda p, c: (0, layer_at, 0, 0)),
            ],
            out_specs=[whole_spec((rows, D)), whole_spec((rows, D)), score_pair],
            scratch_shapes=[
                pltpu.VMEM((2, rows, length), jnp.float32),
                pltpu.VMEM((2, rows, length), jnp.bfloat16),
            ],
        ),
        out_shape=[
            jax.ShapeDtypeStruct((rows, D), jnp.bfloat16),
            jax.ShapeDtypeStruct((rows, D), jnp.float32),
            jax.ShapeDtypeStruct((HEADS, rows, length), jnp.float32),
        ],
        compiler_params=pltpu.CompilerParams(vmem_limit_bytes=VMEM_LIMIT),
        cost_estimate=COST,
        name="attend",
    )(count, query, key_t, value, squery, skey_t, bias, out_w)


def attend_back_kernel(
    tile,
    *refs,
):
    (query_ref, key_ref, value_ref, squery_ref, skey_ref, grad_ref), refs = refs[:6], refs[6:]
    attn_ref, refs = refs[0], refs[1:]
    prob_refs, (out_ref, score_out_ref, dprob_ref, prob_low_ref) = refs[:-4], refs[-4:]
    rows = prob_refs[0].shape[1]
    lanes = lax.broadcasted_iota(jnp.int32, (1, 2 * HD), 1)
    queries = jnp.concatenate([query_ref[...], squery_ref[...]], axis=1)
    keys = jnp.concatenate([key_ref[...], skey_ref[...]], axis=1)
    grads = grad_ref[...]
    results = []
    for half in range(2):
        own = low(((lanes >= HD) == (half == 1)).astype(jnp.float32))
        dprob_ref[...] = dot(grads * own, value_ref[...])
        for chunk, prob_ref in enumerate(prob_refs):

            def group(step, carry, chunk=chunk, prob_ref=prob_ref):
                span = pl.ds(pl.multiple_of(step * tile, tile), tile)
                there = pl.ds(pl.multiple_of(chunk * rows + step * tile, tile), tile)
                prob = prob_ref[half, span, :]
                dprob = dprob_ref[there, :]
                total = jnp.sum(prob * dprob, axis=1, keepdims=True)
                score_out_ref[half, there, :] = low(prob * (dprob - total))
                prob_low_ref[there, :] = low(prob)
                return carry

            lax.fori_loop(0, rows // tile, group, 0)
        scores = score_out_ref[half]
        results.append(
            (
                dot(scores, keys) * SCALE,
                dot(scores, queries, 0, 0) * SCALE,
                dot(prob_low_ref[...], grads, 0, 0),
            )
        )
    (dq0, dk0, dv0), (dq1, dk1, dv1) = results
    upper = lanes >= HD
    wide = 2 * HD
    out_ref[0] = low(jnp.where(upper, dq1[:, :wide], dq0[:, :wide]))
    out_ref[1] = low(jnp.where(upper, dk1[:, :wide], dk0[:, :wide]))
    out_ref[2] = low(jnp.where(upper, dv1, dv0))
    out_ref[3] = low(jnp.where(upper, dq1[:, wide:], dq0[:, wide:]))
    out_ref[4] = low(jnp.where(upper, dk1[:, wide:], dk0[:, wide:]))
    out_ref[5] = attn_ref[...]


def attend_back(clock, projected, probs, context_grad, attn_low):
    query, key, value_t, squery, skey = projected
    length = query.shape[0]
    pair = pl.BlockSpec((length, 2 * HD), lambda p: (0, p))
    value_pair = pl.BlockSpec((2 * HD, length), lambda p: (p, 0))
    prob_specs = [pl.BlockSpec((2,) + prob.shape[1:], lambda p: (p, 0, 0)) for prob in probs]
    return clock.call(
        partial(attend_back_kernel, 128),
        [
            jax.ShapeDtypeStruct((6, length, D), jnp.bfloat16),
            jax.ShapeDtypeStruct((HEADS, length, length), jnp.bfloat16),
        ],
        [query, key, value_t, squery, skey, context_grad, attn_low, *probs],
        [pair, pair, value_pair, pair, pair, pair, pair] + prob_specs,
        [
            pl.BlockSpec((6, length, 2 * HD), lambda p: (0, 0, p)),
            pl.BlockSpec((2, length, length), lambda p: (p, 0, 0)),
        ],
        (HEADS // 2,),
        "attend_back",
        [
            pltpu.VMEM((length, length), jnp.float32),
            pltpu.VMEM((length, length), jnp.bfloat16),
        ],
    )


def bucket_kernel(one_ref, two_ref, grad_ref, out_ref, sum_ref):
    step = pl.program_id(0)
    group, length = one_ref.shape
    buckets = NB1 + NB2

    @pl.when(step == 0)
    def clear():
        sum_ref[...] = jnp.zeros_like(sum_ref)

    first_ids = lax.broadcasted_iota(jnp.int32, (NB1, 1), 0)
    second_ids = lax.broadcasted_iota(jnp.int32, (NB2, 1), 0)
    hot = []
    for row in range(group):
        hot.append(low((one_ref[row : row + 1, :] == first_ids).astype(jnp.float32)))
        hot.append(low((two_ref[row : row + 1, :] == second_ids).astype(jnp.float32)))
    hot = jnp.concatenate(hot, axis=0)
    grads = grad_ref[...].reshape(HEADS * group, length)
    sum_ref[...] += dot(hot, grads, 1, 1)

    @pl.when(step == pl.num_programs(0) - 1)
    def finish():
        member = lax.broadcasted_iota(jnp.int32, (1, HEADS * group), 1) % group
        total = jnp.zeros((buckets, HEADS * group), jnp.float32)
        for row in range(group):
            block = sum_ref[row * buckets : (row + 1) * buckets, :]
            total = total + jnp.where(member == row, block, 0.0)
        out_ref[...] = total


def bucket_sums(clock, rel_one, rel_two, score_grad):
    length = rel_one.shape[0]
    group = 16
    buckets = NB1 + NB2
    rel = pl.BlockSpec((group, length), lambda i: (i, 0))
    sums = clock.call(
        bucket_kernel,
        jax.ShapeDtypeStruct((buckets, HEADS * group), jnp.float32),
        [rel_one, rel_two, score_grad],
        [rel, rel, pl.BlockSpec((HEADS, group, length), lambda i: (0, i, 0))],
        whole_spec((buckets, HEADS * group)),
        (length // group,),
        "bucket_sums",
        [pltpu.VMEM((group * buckets, HEADS * group), jnp.float32)],
    )
    return jnp.sum(sums.reshape(buckets, HEADS, group), axis=2).T


def dp_strides(size):
    return tuple(1 << place for place in range(size.bit_length() - 1))


def orders(size):
    rest = dp_strides(size)[1:]
    if len(rest) < 2:
        return rest, rest
    return rest, (rest[1], rest[0]) + rest[2:]


def place(relative, order):
    spot = relative * 0
    for stride in order:
        spot = spot * 2 + (relative // (stride // 2)) % 2
    return spot


def rows_kernel(parts, order, ends, me_ref, *refs):
    left_refs, (right_ref, send_ref, keep_ref, sum_ref) = refs[:-4], refs[-4:]
    width = sum_ref.shape[0] // parts
    step = pl.program_id(0)
    right = right_ref[...].reshape(right_ref.shape[-2:])
    for index, left_ref in enumerate(left_refs):
        start = ends[index - 1] if index else 0

        @pl.when((step >= start) & (step < ends[index]))
        def product(left_ref=left_ref):
            sum_ref[...] = dot(left_ref[...], right, 0, 0)

    me = me_ref[0]
    core = me % 2
    for block in range(parts // 2):
        spot = place(jnp.bitwise_xor(block, me // 2), order)
        own = pl.ds(pl.multiple_of((2 * block + core) * width, 8), width)
        other = pl.ds(pl.multiple_of((2 * block + 1 - core) * width, 8), width)
        shape = (1,) * (len(keep_ref.shape) - 2) + (width, sum_ref.shape[1])
        keep_ref[pl.ds(spot, 1)] = sum_ref[own, :].reshape(shape)
        send_ref[pl.ds(spot, 1)] = sum_ref[other, :].reshape(shape)


def pair_kernel(me_ref, left_ref, right_ref, send_ref, keep_ref, sum_ref):
    width = sum_ref.shape[0] // 2
    sum_ref[...] = dot(left_ref[...], right_ref[...], 0, 0)
    core = me_ref[0] % 2
    own = pl.ds(pl.multiple_of(core * width, 8), width)
    other = pl.ds(pl.multiple_of((1 - core) * width, 8), width)
    keep_ref[0] = sum_ref[own, :]
    send_ref[0] = sum_ref[other, :]


def natural_blocks(values, me, size, order):
    blocks = values.reshape((size // 2, 2) + (values.shape[0] // size,) + values.shape[1:])
    spots = jnp.arange(size // 2, dtype=jnp.int32)
    relative = spots * 0
    for rank, stride in enumerate(reversed(order)):
        relative = relative + (spots >> rank) % 2 * (stride // 2)
    blocks = jnp.take(blocks, jnp.bitwise_xor(relative, me // 2), axis=0)
    core = me % 2
    own = lax.dynamic_index_in_dim(blocks, core, 1, keepdims=False)
    other = lax.dynamic_index_in_dim(blocks, 1 - core, 1, keepdims=False)
    return other, own


def wide_grad(clock, left, right, me, size, order):
    length, rows = left.shape
    wide = right.shape[1]
    width = rows // size
    if width % 8:
        return natural_blocks(dot(left, right, 0, 0), me[0], size, order)
    step = D
    half = size // 2
    block = pl.BlockSpec((half, width, step), lambda j, m: (0, 0, j))
    shape = jax.ShapeDtypeStruct((half, width, wide), jnp.float32)
    return clock.call(
        partial(rows_kernel, size, order, (wide // step,)),
        [shape, shape],
        [left, right],
        [whole_spec(left.shape), pl.BlockSpec((length, step), lambda j, m: (0, j))],
        [block, block],
        (wide // step,),
        "wide_grad",
        [pltpu.VMEM((rows, step), jnp.float32)],
        [me],
    )


def proj_grad(clock, lefts, right, first, me, size, order):
    length, rows = lefts[0][0].shape
    ends = []
    for left, count in lefts:
        ends.append(count + (ends[-1] if ends else 0))
    width = rows // size
    if width % 8:
        used = [left for left, count in lefts for at in range(count)]
        parts = jnp.stack([dot(left, right[first + j], 0, 0) for j, left in enumerate(used)])
        blocks = natural_blocks(jnp.swapaxes(parts, 0, 1), me[0], size, order)
        return [jnp.swapaxes(part, 1, 2) for part in blocks]
    half = size // 2
    block = pl.BlockSpec((half, 1, width, D), lambda j, m: (0, j, 0, 0))
    shape = jax.ShapeDtypeStruct((half, ends[-1], width, D), jnp.float32)
    return clock.call(
        partial(rows_kernel, size, order, tuple(ends)),
        [shape, shape],
        [left for left, count in lefts] + [right],
        [whole_spec((length, rows)) for left in lefts]
        + [pl.BlockSpec((1, length, D), lambda j, m: (first + j, 0, 0))],
        [block, block],
        (ends[-1],),
        "proj_grad",
        [pltpu.VMEM((rows, D), jnp.float32)],
        [me],
    )


def tall_grad(clock, left, right, me, size, order):
    length, rows = left.shape
    wide = right.shape[1]
    width = rows // size
    if width % 8 or 2 * width % LANES:
        return natural_blocks(dot(left, right, 0, 0), me[0], size, order)
    half = size // 2
    block = pl.BlockSpec(
        (1, width, wide), lambda i, m: (place(jnp.bitwise_xor(i, m[0] // 2), order), 0, 0)
    )
    shape = jax.ShapeDtypeStruct((half, width, wide), jnp.float32)
    return clock.call(
        pair_kernel,
        [shape, shape],
        [left, right],
        [pl.BlockSpec((length, 2 * width), lambda i, m: (0, i)), whole_spec(right.shape)],
        [block, block],
        (half,),
        "tall_grad",
        [pltpu.VMEM((2 * width, wide), jnp.float32)],
        [me],
    )


def swap_dp(values, stride, size):
    return lax.ppermute(values, "dp", [(index, index ^ stride) for index in range(size)])


def add_kernel(*refs):
    total = refs[0][...]
    for ref in refs[1:-1]:
        total = total + ref[...]
    refs[-1][...] = total


def add_blocks(clock, parts, first, count):
    shape = parts[0].shape[1:]
    tail = (0,) * len(shape)
    return clock.call(
        add_kernel,
        jax.ShapeDtypeStruct((count,) + shape, jnp.float32),
        parts,
        [pl.BlockSpec((1,) + shape, lambda i: (first + i,) + tail)] * len(parts),
        pl.BlockSpec((1,) + shape, lambda i: (i,) + tail),
        (count,),
        "add_blocks",
    )


class Reduction:
    def __init__(self, clock, blocks, order, size):
        self.clock = clock
        self.size = size
        self.order = list(order)
        send, keep = blocks
        self.parts = [keep, swap_dp(send, 1, size)]
        self.left = keep.shape[0]
        self.total = None

    def advance(self):
        if not self.order:
            self.total = add_blocks(self.clock, self.parts, 0, 1)[0]
            return
        self.left //= 2
        sent = add_blocks(self.clock, self.parts, self.left, self.left)
        self.parts.append(swap_dp(sent, self.order.pop(0), self.size))

    def finish(self):
        while self.total is None:
            self.advance()
        return self.total


def bins_kernel(half, at_ref, boxes_ref, grad_ref, send_ref, keep_ref):
    step = pl.program_id(0)
    width = keep_ref.shape[1]
    for ref, spot in ((keep_ref, step), (send_ref, step + half)):
        block = jnp.bitwise_xor(spot, at_ref[0])
        table = block // half
        ids = lax.broadcasted_iota(jnp.int32, (width, 1), 0) + (block - table * half) * width
        hot = low((boxes_ref[pl.ds(table, 1), :] == ids).astype(jnp.float32))
        ref[0] = dot(hot, grad_ref[...])


def table_grad(clock, boxes, grad, bins, at, parts):
    half = parts // 2
    width = 2 * bins // parts
    block = pl.BlockSpec((1, width, D), lambda i, m: (i, 0, 0))
    shape = jax.ShapeDtypeStruct((half, width, D), jnp.float32)
    return clock.call(
        partial(bins_kernel, half),
        [shape, shape],
        [boxes, grad],
        [whole_spec(boxes.shape), whole_spec(grad.shape)],
        [block, block],
        (half,),
        "table_grad",
        (),
        [at],
    )


def join_kernel(starts, *refs):
    step = pl.program_id(0)
    for part, ref in enumerate(refs[:-1]):

        @pl.when((step >= starts[part]) & (step < starts[part + 1]))
        def copy(ref=ref):
            refs[-1][...] = ref[...]


def join(clock, parts, at=None):
    starts = [0]
    for part in parts:
        starts.append(starts[-1] + part.shape[0])
    shape = parts[0].shape[1:]
    mask = starts[-1] - 1

    def spec(index):
        start, count = starts[index], parts[index].shape[0]
        return pl.BlockSpec((1,) + shape, lambda i, *m: (jnp.clip(i - start, 0, count - 1), 0, 0))

    def kernel(*refs):
        join_kernel(starts, *(refs if at is None else refs[1:]))

    def spot(i, *m):
        return (i if at is None else jnp.bitwise_xor(i, m[0][0] & mask), 0, 0)

    return clock.call(
        kernel,
        jax.ShapeDtypeStruct((starts[-1],) + shape, jnp.float32),
        parts,
        [spec(index) for index in range(len(parts))],
        pl.BlockSpec((1,) + shape, spot),
        (starts[-1],),
        "join",
        (),
        () if at is None else [at],
    )


def halves_kernel(core_ref, own_ref, other_ref, out_ref):
    here = pl.program_id(0) == core_ref[0]

    @pl.when(here)
    def own():
        out_ref[0] = own_ref[...]

    @pl.when(jnp.logical_not(here))
    def other():
        out_ref[0] = other_ref[...]


def halves(clock, own, other, core):
    step = 4
    count = own.shape[0] // step
    block = (step,) + own.shape[1:]

    def spec(mine):
        def spot(half, i, c):
            here = (half == c[0]) if mine else (half != c[0])
            return (jnp.where(here, i, jnp.where(half == 0, 0, count - 1)), 0, 0)

        return pl.BlockSpec(block, spot)

    return clock.call(
        halves_kernel,
        jax.ShapeDtypeStruct((2,) + own.shape, jnp.float32),
        [own, other],
        [spec(True), spec(False)],
        pl.BlockSpec((1,) + block, lambda half, i, c: (half, i, 0, 0)),
        (2, count),
        "halves",
        (),
        [core],
    )


class EverySum:
    def __init__(self, clock, boxes, grad, bins, size):
        self.clock = clock
        self.size = size
        strides = dp_strides(size)
        self.steps = [strides[0], None] + list(strides[1:])
        dp_at = lax.axis_index("dp")
        at = dp_at * 0
        for stride in self.steps:
            bit = lax.axis_index("stream") if stride is None else dp_at // stride % 2
            at = at * 2 + bit
        self.at = at.astype(jnp.int32).reshape(1)
        send, keep = table_grad(clock, boxes, grad, bins, self.at, 2 * size)
        self.parts = [keep, self.swap(send, self.steps[0])]
        self.left = size
        self.down = self.steps[1:]
        self.up = list(reversed(self.steps))

    def swap(self, values, stride):
        if stride is None:
            return lax.ppermute(values, "stream", SWAP)
        return swap_dp(values, stride, self.size)

    def advance(self):
        if self.down:
            self.left //= 2
            sent = add_blocks(self.clock, self.parts, self.left, self.left)
            self.parts.append(self.swap(sent, self.down.pop(0)))
        elif self.up:
            if self.left:
                self.parts = [add_blocks(self.clock, self.parts, 0, 1)]
                self.left = 0
                sent = self.parts[0]
            else:
                at = self.at if len(self.up) == 1 else None
                sent = join(self.clock, self.parts, at)
                self.parts = [sent]
            self.parts.append(self.swap(sent, self.up.pop(0)))

    def finish(self):
        while self.down or self.up:
            self.advance()
        return halves(self.clock, *self.parts, self.at // self.size)


class SmallSum:
    def __init__(self, clock, values, size):
        self.clock = clock
        self.size = size
        self.parts = [values[None]]
        self.strides = list(dp_strides(size))

    def advance(self):
        if len(self.parts) > 1:
            self.parts = [add_blocks(self.clock, self.parts, 0, 1)]
        if self.strides:
            self.parts.append(swap_dp(self.parts[0], self.strides.pop(0), self.size))

    def finish(self):
        while len(self.parts) > 1:
            self.advance()
        return self.parts[0][0]


def norm_back(grad, normal, root, gain):
    scaled = grad * gain
    inner = jnp.mean(scaled * normal, axis=-1, keepdims=True)
    outer = jnp.mean(scaled, axis=-1, keepdims=True)
    return (scaled - outer - normal * inner) * root


def norm_sums(grad, normal):
    return jnp.concatenate(
        [
            jnp.sum(grad * normal, axis=0, keepdims=True),
            jnp.sum(grad, axis=0, keepdims=True),
            jnp.zeros((6, grad.shape[1]), jnp.float32),
        ],
        axis=0,
    )


def second_kernel(grad_ref, normal_ref, root_ref, gain_ref, back_ref, low_ref, sums_ref):
    @pl.when(pl.program_id(0) == 0)
    def clear():
        sums_ref[...] = jnp.zeros_like(sums_ref)

    grad = grad_ref[...]
    back = norm_back(grad, normal_ref[...], root_ref[...], gain_ref[...])
    back_ref[...] = back
    low_ref[...] = low(back)
    sums_ref[...] += norm_sums(grad, normal_ref[...])


def second_back(clock, grad, normal, root, gain):
    length = grad.shape[0]
    step = 128
    rows = pl.BlockSpec((step, D), lambda i: (i, 0))
    return clock.call(
        second_kernel,
        [
            jax.ShapeDtypeStruct((length, D), jnp.float32),
            jax.ShapeDtypeStruct((length, D), jnp.bfloat16),
            jax.ShapeDtypeStruct((8, D), jnp.float32),
        ],
        [grad, normal, root, gain[None]],
        [rows, rows, pl.BlockSpec((step, 1), lambda i: (i, 0)), whole_spec((1, D))],
        [rows, rows, whole_spec((8, D))],
        (length // step,),
        "second_back",
    )


def inner_kernel(branch_ref, w_ref, inner_ref, out_ref):
    act_grad = dot(branch_ref[...], w_ref[...], 1, 1)
    inner = inner_ref[...]
    slope = 0.5 * (1.0 + lax.erf(inner * SQRT_HALF)) + inner * (
        DENSITY * jnp.exp(-0.5 * inner * inner)
    )
    out_ref[...] = low(act_grad * slope)


def inner_back(clock, branch_low, w_out, at, inner):
    length, wide = inner.shape
    step = 512
    cols = pl.BlockSpec((length, step), lambda j: (0, j))
    return clock.call(
        inner_kernel,
        jax.ShapeDtypeStruct((length, wide), jnp.bfloat16),
        [branch_low, w_out, inner],
        [
            whole_spec(branch_low.shape),
            pl.BlockSpec((None, None, step, D), lambda j: (0, at, j, 0)),
            cols,
        ],
        cols,
        (wide // step,),
        "inner_back",
    )


def first_kernel(
    inner_ref, w_ref, back_ref, normal_ref, root_ref, gain_ref, out_ref, sums_ref, sum_ref
):
    step = pl.program_id(0)
    part = dot(inner_ref[...], w_ref[...], 1, 1)

    @pl.when(step == 0)
    def start():
        sum_ref[...] = back_ref[...] + part

    @pl.when(step > 0)
    def more():
        sum_ref[...] += part

    @pl.when(step == pl.num_programs(0) - 1)
    def finish():
        tile = 128
        sums = jnp.zeros((8, D), jnp.float32)
        for at in range(0, sum_ref.shape[0], tile):
            span = slice(at, at + tile)
            grad = sum_ref[span, :]
            out_ref[span, :] = norm_back(
                grad, normal_ref[span, :], root_ref[span, :], gain_ref[...]
            )
            sums = sums + norm_sums(grad, normal_ref[span, :])
        sums_ref[...] = sums


def first_back(clock, inner_low, w_in, at, sum_grad, normal, root, gain):
    length, wide = inner_low.shape
    step = 768
    return clock.call(
        first_kernel,
        [
            jax.ShapeDtypeStruct((length, D), jnp.float32),
            jax.ShapeDtypeStruct((8, D), jnp.float32),
        ],
        [inner_low, w_in, sum_grad, normal, root, gain[None]],
        [
            pl.BlockSpec((length, step), lambda j: (0, j)),
            pl.BlockSpec((None, None, D, step), lambda j: (0, at, 0, j)),
            whole_spec((length, D)),
            whole_spec((length, D)),
            whole_spec((length, 1)),
            whole_spec((1, D)),
        ],
        [whole_spec((length, D)), whole_spec((8, D))],
        (wide // step,),
        "first_back",
        [pltpu.VMEM((length, D), jnp.float32)],
    )


def context_kernel(count_ref, own_ref, other_ref, w_ref, out_ref, attn_ref):
    rows = own_ref.shape[0]
    mask = (lax.broadcasted_iota(jnp.int32, (rows, 1), 0) < count_ref[0]).astype(jnp.float32)
    attn = low((own_ref[...] + other_ref[...]) * mask)
    attn_ref[...] = attn
    out_ref[...] = low(dot(attn, w_ref[...], 1, 1))


def context_back(clock, count, own, other, out_w, at):
    shape = jax.ShapeDtypeStruct(own.shape, jnp.bfloat16)
    return clock.call(
        context_kernel,
        [shape, shape],
        [own, other, out_w],
        [
            whole_spec(own.shape),
            whole_spec(own.shape),
            pl.BlockSpec((None, None, D, D), lambda i, c: (0, at, 0, 0)),
        ],
        [whole_spec(own.shape), whole_spec(own.shape)],
        (1,),
        "context_back",
        (),
        [count],
    )


def input_kernel(grad_ref, w_ref, start_ref, out_ref):
    step = pl.program_id(0)
    part = dot(grad_ref[0], w_ref[0], 1, 1)

    @pl.when(step == 0)
    def start():
        out_ref[...] = start_ref[...] + part

    @pl.when(step > 0)
    def more():
        out_ref[...] += part


def input_back(clock, grads, weights, at, start, first, count):
    length = grads.shape[1]
    return clock.call(
        input_kernel,
        jax.ShapeDtypeStruct(start.shape, jnp.float32),
        [grads, weights, start],
        [
            pl.BlockSpec((1, length, D), lambda j: (first + j, 0, 0)),
            pl.BlockSpec((None, None, 1, D, D), lambda j: (0, at, first + j, 0, 0)),
            whole_spec(start.shape),
        ],
        whole_spec(start.shape),
        (count,),
        "input_back",
    )


def normalize(values):
    center = values - jnp.mean(values, axis=-1, keepdims=True)
    root = lax.rsqrt(jnp.mean(center * center, axis=-1, keepdims=True) + EPS)
    return center * root, root


def swap_stream(values):
    return lax.ppermute(values, "stream", SWAP)


def layer_forward(hidden, spatial, weights, out_w, layer_at, biases, count, pause):
    projections, w_in, w_out, gains, shifts = weights
    length = hidden.shape[0]
    chunks = len(biases)
    rows = length // chunks
    rounded = low(hidden)
    projected = (
        low(dot(rounded, projections[0])),
        low(dot(projections[1], rounded, 0, 1)),
        low(dot(rounded, projections[2])),
        low(dot(spatial, projections[3])),
        low(dot(projections[4], spatial, 0, 1)),
    )
    contexts, mixed, probs = [], [], []
    last = None
    for at in range(chunks):
        bias = biases[at]
        bias = bias(last) if callable(bias) else bias
        context, attn, prob = attend(count, projected, bias, out_w, layer_at, at, rows)
        contexts.append(context)
        mixed.append(attn + swap_stream(attn))
        probs.append(prob)
        last = attn
    extra = pause(last)
    mixed = jnp.concatenate(mixed, axis=0)
    if extra is not None:
        mixed = gate(mixed, *extra)
    first_normal, first_root = normalize(hidden + mixed)
    normed = first_normal * gains[0] + shifts[0]
    normed_low = low(normed)
    inner = dot(normed_low, w_in)
    activated = low(0.5 * inner * (1.0 + lax.erf(inner * SQRT_HALF)))
    second_normal, second_root = normalize(normed + dot(activated, w_out))
    result = second_normal * gains[1] + shifts[1]
    kept = (
        rounded,
        projected,
        jnp.concatenate(contexts, axis=0),
        probs,
        (first_normal, first_root),
        normed_low,
        inner,
        activated,
        (second_normal, second_root),
    )
    return result, kept, extra


def local(
    dp_size,
    tokens,
    boxes,
    rel_one,
    rel_two,
    vis_count,
    spatial_tables,
    proj_weights,
    out_weights,
    ffn_in,
    ffn_out,
    norm_gains,
    norm_shifts,
    bias_tables,
    cotangent,
):
    length = tokens.shape[2]
    stream_at = lax.axis_index("stream")
    me = lax.axis_index("dp").astype(jnp.int32).reshape(1)
    count = jnp.where(stream_at == 0, length, vis_count).astype(jnp.int32)
    rowmask = (jnp.arange(length, dtype=jnp.int32)[:, None] < count[0]).astype(jnp.float32)
    rel = (rel_one[0, 0], rel_two[0, 0])
    bin_ids = jnp.arange(spatial_tables.shape[1], dtype=jnp.int32)
    hot_x = low(boxes[0, 0, 0][:, None] == bin_ids[None, :])
    hot_y = low(boxes[0, 0, 1][:, None] == bin_ids[None, :])
    spatial = low(dot(hot_x, spatial_tables[0]) + dot(hot_y, spatial_tables[1]))
    tables = bias_tables[0].astype(jnp.float32)
    tables = jnp.stack(
        [
            jnp.pad(tables[:, :, :NB1], ((0, 0), (0, 0), (0, LANES - NB1))),
            jnp.pad(tables[:, :, NB1:], ((0, 0), (0, 0), (0, LANES - NB2))),
        ],
        axis=1,
    )

    def layer_weights(layer_at):
        return (
            proj_weights[0, layer_at],
            ffn_in[0, layer_at],
            ffn_out[0, layer_at],
            norm_gains[0, layer_at],
            norm_shifts[0, layer_at],
        )

    chunks = 2
    rows = length // chunks

    def bias_of(layer_at, at):
        def make(last):
            ones = rel[0] if last is None else gate(rel[0], last)
            return score_bias(ones, rel[1], tables[layer_at], at, rows)

        return make

    hidden = tokens[0, 0].astype(jnp.float32)
    kept = []
    biases = [bias_of(0, at) for at in range(chunks)]
    for layer_at in range(LAYERS):

        def pause(last, layer_at=layer_at):
            if layer_at + 1 == LAYERS:
                return None
            return [bias_of(layer_at + 1, at)(last) for at in range(chunks)]

        hidden, state, biases = layer_forward(
            hidden, spatial, layer_weights(layer_at), out_weights, layer_at, biases, count, pause
        )
        kept.append(state)
    output = low(hidden * rowmask)[None, None]

    grad = cotangent[0, 0].astype(jnp.float32) * rowmask
    clock = Order()
    both_orders = orders(dp_size)
    step_order = {
        name + layer: both_orders[name + layer in NEAR]
        for name in ("tall", "wide", "token", "place")
        for layer in "01"
    }
    moves = {}
    state = {"grad1": grad}

    def move(name, blocks):
        moves[name] = Reduction(clock, blocks, step_order[name], dp_size)

    def second(layer):
        gains = norm_gains[0, int(layer)]
        normal, root = kept[int(layer)][8]
        results = second_back(clock, state["grad" + layer], normal, root, gains[1])
        state["sum" + layer], state["branch" + layer], state["second_sums" + layer] = results

    def tall(layer):
        activated = kept[int(layer)][7]
        name = "tall" + layer
        move(name, tall_grad(clock, activated, state["branch" + layer], me, dp_size, step_order[name]))

    def inner(layer):
        state["inner" + layer] = inner_back(
            clock, state["branch" + layer], ffn_out, int(layer), kept[int(layer)][6]
        )

    def wide(layer):
        normed_low = kept[int(layer)][5]
        name = "wide" + layer
        move(name, wide_grad(clock, normed_low, state["inner" + layer], me, dp_size, step_order[name]))

    def first(layer):
        normal, root = kept[int(layer)][4]
        gains = norm_gains[0, int(layer)]
        state["first" + layer], state["first_sums" + layer] = first_back(
            clock,
            state["inner" + layer],
            ffn_in,
            int(layer),
            state["sum" + layer],
            normal,
            root,
            gains[0],
        )
        state["other" + layer] = swap_stream(state["first" + layer])

    def context(layer):
        state["context" + layer], state["attn" + layer] = context_back(
            clock, count, state["first" + layer], state["other" + layer], out_weights, int(layer)
        )

    def attention(layer):
        query, key_t, value, squery, skey_t = kept[int(layer)][1]
        state["proj" + layer], state["scores" + layer] = attend_back(
            clock,
            (query, key_t.T, value.T, squery, skey_t.T),
            kept[int(layer)][3],
            state["context" + layer],
            state["attn" + layer],
        )

    def token(layer):
        lefts = [(kept[int(layer)][0], 3)]
        name = "token" + layer
        move(name, proj_grad(clock, lefts, state["proj" + layer], 0, me, dp_size, step_order[name]))

    def place_step(layer):
        lefts = [(spatial, 2), (kept[int(layer)][2], 1)]
        name = "place" + layer
        move(name, proj_grad(clock, lefts, state["proj" + layer], 3, me, dp_size, step_order[name]))

    def dx(layer):
        grad = input_back(
            clock, state["proj" + layer], proj_weights, int(layer), state["first" + layer], 0, 3
        )
        state["grad" + str(int(layer) - 1)] = grad

    def space(layer):
        last = int(layer) + 1 == LAYERS
        start = jnp.zeros((length, D), jnp.float32) if last else state["space" + str(int(layer) + 1)]
        state["space" + layer] = input_back(
            clock, state["proj" + layer], proj_weights, int(layer), start, 3, 2
        )

    bins = spatial_tables.shape[1]

    def table(layer):
        moves["all0"] = EverySum(clock, boxes[0, 0], low(state["space0"]), bins, dp_size)

    def bucket(layer):
        state["buckets" + layer] = bucket_sums(clock, rel[0], rel[1], state["scores" + layer])

    def tiny(layer):
        norms = []
        for at in "01":
            sums = (state["first_sums" + at], state["second_sums" + at])
            norms += [sums[0][0], sums[1][0], sums[0][1], sums[1][1]]
        buckets = [state["buckets" + at] for at in "01"]
        flat = jnp.concatenate(
            [part.reshape(-1, LANES) for part in (jnp.stack(norms), jnp.stack(buckets))], axis=0
        )
        moves["norms0"] = SmallSum(clock, flat, dp_size)

    kernels = (
        second,
        tall,
        inner,
        wide,
        first,
        context,
        attention,
        token,
        place_step,
        dx,
        space,
        table,
        bucket,
        tiny,
    )
    for step in PLAN:
        name, layer = step // 2, str(step % 2)
        if name < len(kernels):
            kernels[name](layer)
        else:
            moves[NAMES[name - len(kernels)] + layer].advance()
    owns = {name: moves[name].finish() for name in step_order}
    layers = "01"
    scattered = (
        jnp.stack([jnp.concatenate([owns["token" + at], owns["place" + at][:2]]) for at in layers]),
        jnp.stack([owns["place" + at][2] for at in layers]),
        jnp.stack([owns["wide" + at] for at in layers]),
        jnp.stack([owns["tall" + at] for at in layers]),
    )
    shared = moves["all0"].finish().reshape(2, bins, D)
    flat = moves["norms0"].finish()
    normed = flat[: 4 * LAYERS * D // LANES].reshape(LAYERS, 4, D)
    width = D // dp_size
    normed = lax.dynamic_slice_in_dim(normed, me[0] * width, width, 2)
    bucket_own = flat[4 * LAYERS * D // LANES :].reshape(1, LAYERS, HEADS, NB1 + NB2)
    return (
        output,
        state["grad-1"][None, None],
        shared,
        *(part[None] for part in scattered),
        normed[None, :, :2],
        normed[None, :, 2:],
        bucket_own,
    )


NAMES = ("tall", "wide", "token", "place", "all", "norms")
(SECOND0, SECOND1, TALL0, TALL1, INNER0, INNER1, WIDE0, WIDE1, FIRST0, FIRST1) = range(10)
(CONTEXT0, CONTEXT1, ATTEND0, ATTEND1, TOKEN0, TOKEN1, PLACE0, PLACE1, DX0, DX1) = range(10, 20)
(SPACE0, SPACE1, TABLE0, TABLE1, BUCKET0, BUCKET1, TINY0, TINY1) = range(20, 28)
(T0, T1, W0, W1, K0, K1, P0, P1, A0, A1, N0, N1) = range(28, 40)
NEAR = ("wide1", "place1",)
PLAN = (
    SECOND1, TALL1, INNER1, WIDE1, FIRST1, T1, W1, CONTEXT1, ATTEND1, T1, TOKEN1, W1, DX1, SECOND0,
    K1, T1, TALL0, INNER0, W1, T1, WIDE0, T0, SPACE1, FIRST0, W1, K1, PLACE1, BUCKET1, CONTEXT0, P1,
    W0, K1, ATTEND0, SPACE0, K1, TABLE0, DX0, P1, A0, W0, P1, A0, W0, P1, TOKEN0, A0, K0, T0, A0,
    W0, PLACE0, A0, P0, A0, T0, BUCKET0, A0, K0, T0, TINY0, P0, A0, N0, N0, K0, P0, A0, N0, K0, N0,
    A0, P0,
)


def solution(mesh):
    placed = (
        P("stream", "dp", None, None),
        P("stream", "dp", None, None),
        P("stream", "dp", None, None),
        P("stream", "dp", None, None),
        P("dp"),
        P(),
        P("stream", None, None, None, None),
        P("stream", None, None, None),
        P("stream", None, None, None),
        P("stream", None, None, None),
        P("stream", None, None, None),
        P("stream", None, None, None),
        P("stream", None, None, None),
        P("stream", "dp", None, None),
    )
    return jax.shard_map(
        partial(local, mesh.shape["dp"]),
        mesh=mesh,
        in_specs=placed,
        out_specs=(
            P("stream", "dp", None, None),
            P("stream", "dp", None, None),
            P(),
            P("stream", None, None, "dp", None),
            P("stream", None, "dp", None),
            P("stream", None, "dp", None),
            P("stream", None, "dp", None),
            P("stream", None, None, "dp"),
            P("stream", None, None, "dp"),
            P("stream", None, None, None),
        ),
        check_vma=False,
    )
```

```python
from functools import partial

import jax
import jax.numpy as jnp
from jax import lax
from jax.experimental import pallas as pl
from jax.experimental.pallas import tpu as pltpu
from jax.sharding import PartitionSpec as P

D = 768
HEADS = 12
HD = 64
NB1 = 32
NB2 = 64
LAYERS = 2
LANES = 128
NEG_FILL = -1e30
EPS = 1e-05
SCALE = HD ** (-0.5)
SQRT_HALF = 0.5**0.5
DENSITY = 0.3989422804014327
SWAP = [(0, 1), (1, 0)]
VMEM_LIMIT = 48 << 20
COST = pl.CostEstimate(flops=10**13, bytes_accessed=10**9, transcendentals=0)


def dot(left, right, left_dim=1, right_dim=0):
    return lax.dot_general(
        left, right, (((left_dim,), (right_dim,)), ((), ())), preferred_element_type=jnp.float32
    )


def low(values):
    return values.astype(jnp.bfloat16)


def gate(values, *deps):
    return lax.optimization_barrier((values,) + deps)[0]


class Order:
    def __init__(self):
        self.last = ()

    def call(
        self,
        kernel,
        shapes,
        operands,
        in_specs,
        out_specs,
        grid,
        name,
        scratch=(),
        scalars=(),
        carried=(),
        mark=0,
    ):
        after = tuple(self.last)
        if any(one is other for one in after for other in carried):
            after = ()
        taken = len(scalars) + len(operands)
        unread = len(carried) + len(after)

        def body(*refs):
            kernel(*refs[:taken], *refs[taken + unread :])

        single = not isinstance(shapes, list)
        results = pl.pallas_call(
            body,
            grid_spec=pltpu.PrefetchScalarGridSpec(
                num_scalar_prefetch=len(scalars),
                grid=grid,
                in_specs=list(in_specs) + [pl.BlockSpec(memory_space=pl.ANY)] * unread,
                out_specs=out_specs,
                scratch_shapes=list(scratch),
            ),
            out_shape=shapes,
            input_output_aliases={taken + at: at for at in range(len(carried))},
            compiler_params=pltpu.CompilerParams(vmem_limit_bytes=VMEM_LIMIT),
            cost_estimate=COST,
            name=name,
        )(*scalars, *operands, *carried, *after)
        self.last = (results if single else results[mark],)
        return results


def whole_spec(shape):
    return pl.BlockSpec(shape, lambda *ids: (0,) * len(shape))


def bias_kernel(one_ref, two_ref, table_ref, bias_ref):
    rows, length = one_ref.shape

    def group(step, carry):
        span = pl.ds(pl.multiple_of(step * 8, 8), 8)
        for col in range(0, length, LANES):
            cols = slice(col, col + LANES)
            first = one_ref[span, cols]
            second = two_ref[span, cols]
            for head in range(HEADS):
                first_row = jnp.broadcast_to(table_ref[0, head : head + 1, :], (8, LANES))
                second_row = jnp.broadcast_to(table_ref[1, head : head + 1, :], (8, LANES))
                bias_ref[head, span, cols] = jnp.take_along_axis(
                    first_row, first, axis=1
                ) + jnp.take_along_axis(second_row, second, axis=1)
        return carry

    lax.fori_loop(0, rows // 8, group, 0)


def score_bias(clock, rel_one, rel_two, table, at, rows):
    length = rel_one.shape[1]
    step = 64
    first = at * rows // step
    rel = pl.BlockSpec((step, length), lambda i: (first + i, 0))
    return clock.call(
        bias_kernel,
        jax.ShapeDtypeStruct((HEADS, rows, length), jnp.float32),
        [rel_one, rel_two, table],
        [rel, rel, whole_spec(table.shape)],
        pl.BlockSpec((HEADS, step, length), lambda i: (0, i, 0)),
        (rows // step,),
        "score_bias",
    )


def attend_kernel(
    at,
    tile,
    count_ref,
    query_ref,
    key_ref,
    value_ref,
    squery_ref,
    skey_ref,
    bias_ref,
    out_w_ref,
    context_ref,
    attn_ref,
    prob_ref,
    score_ref,
    low_ref,
):
    pair = pl.program_id(0)
    rows = query_ref.shape[0]
    length = value_ref.shape[0]
    lanes = lax.broadcasted_iota(jnp.int32, (1, 2 * HD), 1)
    valid = lax.broadcasted_iota(jnp.int32, (1, length), 1) < count_ref[0]
    keys = jnp.concatenate([key_ref[...], skey_ref[...]], axis=0)
    for half in range(2):
        keep = low(((lanes >= HD) == (half == 1)).astype(jnp.float32) * SCALE)
        queries = jnp.concatenate([query_ref[...] * keep, squery_ref[...] * keep], axis=1)
        score_ref[half] = dot(queries, keys)

    def group(step, carry):
        span = pl.ds(pl.multiple_of(step * tile, tile), tile)
        for half in range(2):
            scores = score_ref[half, span, :] + bias_ref[half, span, :]
            scores = jnp.where(valid, scores, NEG_FILL)
            weights = jnp.exp(scores - jnp.max(scores, axis=1, keepdims=True))
            prob = weights * (1.0 / jnp.sum(weights, axis=1, keepdims=True))
            prob_ref[half, span, :] = prob
            low_ref[half, span, :] = low(prob)
        return carry

    lax.fori_loop(0, rows // tile, group, 0)
    first = dot(low_ref[0], value_ref[...])
    second = dot(low_ref[1], value_ref[...])
    cols = pl.ds(pl.multiple_of(pair * 2 * HD, 2 * HD), 2 * HD)
    context_ref[:, cols] = low(jnp.where(lanes >= HD, second, first))

    @pl.when(pair == pl.num_programs(0) - 1)
    def finish():
        index = lax.broadcasted_iota(jnp.int32, (rows, 1), 0) + at * rows
        mask = (index < count_ref[0]).astype(jnp.float32)
        attn_ref[...] = dot(context_ref[...], out_w_ref[...]) * mask


def project_kernel(flipped, left_ref, w_ref, out_ref, flip_ref):
    step = pl.program_id(0)
    result = low(dot(left_ref[...], w_ref[...]))
    out_ref[...] = result

    @pl.when(step >= flipped)
    def flip():
        flip_ref[...] = result.T


def project(clock, left, weights, layer_at, first, count, flipped):
    length = left.shape[0]
    return clock.call(
        partial(project_kernel, flipped),
        [
            jax.ShapeDtypeStruct((count, length, D), jnp.bfloat16),
            jax.ShapeDtypeStruct((count - flipped, D, length), jnp.bfloat16),
        ],
        [left, weights],
        [
            whole_spec((length, D)),
            pl.BlockSpec((None, None, None, D, D), lambda j: (0, layer_at, first + j, 0, 0)),
        ],
        [
            pl.BlockSpec((None, length, D), lambda j: (j, 0, 0)),
            pl.BlockSpec((None, D, length), lambda j: (jnp.maximum(j - flipped, 0), 0, 0)),
        ],
        (count,),
        "project",
    )


def attend(clock, count, projected, bias, out_w, layer_at, at, rows, carried):
    tokens, tokens_t, places, places_t = projected
    length = tokens.shape[1]
    row_pair = pl.BlockSpec((None, rows, 2 * HD), lambda p, c: (0, at, p))
    key_pair = pl.BlockSpec((None, 2 * HD, length), lambda p, c: (0, p, 0))
    value_pair = pl.BlockSpec((None, length, 2 * HD), lambda p, c: (2, 0, p))
    score_pair = pl.BlockSpec((2, rows, length), lambda p, c: (p, 0, 0))
    return clock.call(
        partial(attend_kernel, at, 128),
        [
            jax.ShapeDtypeStruct((length, D), jnp.bfloat16),
            jax.ShapeDtypeStruct((rows, D), jnp.float32),
            jax.ShapeDtypeStruct((HEADS, rows, length), jnp.float32),
        ],
        [tokens, tokens_t, tokens, places, places_t, bias, out_w],
        [
            row_pair,
            key_pair,
            value_pair,
            row_pair,
            key_pair,
            score_pair,
            pl.BlockSpec((None, None, D, D), lambda p, c: (0, layer_at, 0, 0)),
        ],
        [pl.BlockSpec((rows, D), lambda p, c: (at, 0)), whole_spec((rows, D)), score_pair],
        (HEADS // 2,),
        "attend",
        [
            pltpu.VMEM((2, rows, length), jnp.float32),
            pltpu.VMEM((2, rows, length), jnp.bfloat16),
        ],
        [count],
        carried,
        1,
    )


def ffn_kernel(
    x_ref,
    own_ref,
    other_ref,
    gain_ref,
    shift_ref,
    w_in_ref,
    w_out_ref,
    result_ref,
    rounded_ref,
    first_ref,
    first_root_ref,
    low_ref,
    inner_ref,
    act_ref,
    second_ref,
    second_root_ref,
    sum_ref,
):
    step = pl.program_id(0)

    @pl.when(step == 0)
    def start():
        normal, root = normalize(
            x_ref[...].astype(jnp.float32) + (own_ref[...] + other_ref[...])
        )
        normed = normal * gain_ref[0:1, :] + shift_ref[0:1, :]
        first_ref[...] = normal
        first_root_ref[...] = root
        low_ref[...] = low(normed)
        sum_ref[...] = normed

    inner = dot(low_ref[...], w_in_ref[...])
    inner_ref[...] = inner
    act = low(0.5 * inner * (1.0 + lax.erf(inner * SQRT_HALF)))
    act_ref[...] = act
    sum_ref[...] += dot(act, w_out_ref[...])

    @pl.when(step == pl.num_programs(0) - 1)
    def finish():
        normal, root = normalize(sum_ref[...])
        second_ref[...] = normal
        second_root_ref[...] = root
        result = normal * gain_ref[1:2, :] + shift_ref[1:2, :]
        result_ref[...] = result
        rounded_ref[...] = low(result)


def feed_forward(clock, x, own, other, gains, shifts, w_in, w_out, layer_at, at, carried):
    length = x.shape[0]
    rows = own.shape[0]
    wide = w_in.shape[-1]
    step = D
    narrow = pl.BlockSpec((rows, D), lambda j: (at, 0))
    thin = pl.BlockSpec((rows, 1), lambda j: (at, 0))
    broad = pl.BlockSpec((rows, step), lambda j: (at, j))

    def shape(columns, kind):
        return jax.ShapeDtypeStruct((length, columns), kind)

    return clock.call(
        ffn_kernel,
        [
            shape(D, jnp.float32),
            shape(D, jnp.bfloat16),
            shape(D, jnp.float32),
            shape(1, jnp.float32),
            shape(D, jnp.bfloat16),
            shape(wide, jnp.float32),
            shape(wide, jnp.bfloat16),
            shape(D, jnp.float32),
            shape(1, jnp.float32),
        ],
        [x, own, other, gains, shifts, w_in, w_out],
        [
            narrow,
            whole_spec((rows, D)),
            whole_spec((rows, D)),
            whole_spec((2, D)),
            whole_spec((2, D)),
            pl.BlockSpec((None, None, D, step), lambda j: (0, layer_at, 0, j)),
            pl.BlockSpec((None, None, step, D), lambda j: (0, layer_at, j, 0)),
        ],
        [narrow, narrow, narrow, thin, narrow, broad, broad, narrow, thin],
        (wide // step,),
        "feed_forward",
        [pltpu.VMEM((rows, D), jnp.float32)],
        (),
        carried,
    )


def attend_back_kernel(
    tile,
    *refs,
):
    (query_ref, key_ref, value_ref, squery_ref, skey_ref, grad_ref), refs = refs[:6], refs[6:]
    attn_ref, refs = refs[0], refs[1:]
    prob_refs, (out_ref, score_out_ref, dprob_ref, prob_low_ref) = refs[:-4], refs[-4:]
    rows = prob_refs[0].shape[1]
    lanes = lax.broadcasted_iota(jnp.int32, (1, 2 * HD), 1)
    queries = jnp.concatenate([query_ref[...], squery_ref[...]], axis=1)
    keys = jnp.concatenate([key_ref[...], skey_ref[...]], axis=1)
    grads = grad_ref[...]
    results = []
    for half in range(2):
        own = low(((lanes >= HD) == (half == 1)).astype(jnp.float32))
        dprob_ref[...] = dot(grads * own, value_ref[...])
        for chunk, prob_ref in enumerate(prob_refs):

            def group(step, carry, chunk=chunk, prob_ref=prob_ref):
                span = pl.ds(pl.multiple_of(step * tile, tile), tile)
                there = pl.ds(pl.multiple_of(chunk * rows + step * tile, tile), tile)
                prob = prob_ref[half, span, :]
                dprob = dprob_ref[there, :]
                total = jnp.sum(prob * dprob, axis=1, keepdims=True)
                score_out_ref[half, there, :] = low(prob * (dprob - total))
                prob_low_ref[there, :] = low(prob)
                return carry

            lax.fori_loop(0, rows // tile, group, 0)
        scores = score_out_ref[half]
        results.append(
            (
                dot(scores, keys) * SCALE,
                dot(scores, queries, 0, 0) * SCALE,
                dot(prob_low_ref[...], grads, 0, 0),
            )
        )
    (dq0, dk0, dv0), (dq1, dk1, dv1) = results
    upper = lanes >= HD
    wide = 2 * HD
    out_ref[0] = low(jnp.where(upper, dq1[:, :wide], dq0[:, :wide]))
    out_ref[1] = low(jnp.where(upper, dk1[:, :wide], dk0[:, :wide]))
    out_ref[2] = low(jnp.where(upper, dv1, dv0))
    out_ref[3] = low(jnp.where(upper, dq1[:, wide:], dq0[:, wide:]))
    out_ref[4] = low(jnp.where(upper, dk1[:, wide:], dk0[:, wide:]))
    out_ref[5] = attn_ref[...]


def attend_back(clock, projected, probs, context_grad, attn_low):
    tokens, tokens_t, places, places_t = projected
    length = tokens.shape[1]
    pair = pl.BlockSpec((length, 2 * HD), lambda p: (0, p))
    first = pl.BlockSpec((None, length, 2 * HD), lambda p: (0, 0, p))
    second = pl.BlockSpec((None, length, 2 * HD), lambda p: (1, 0, p))
    value_pair = pl.BlockSpec((None, 2 * HD, length), lambda p: (1, p, 0))
    prob_specs = [pl.BlockSpec((2,) + prob.shape[1:], lambda p: (p, 0, 0)) for prob in probs]
    return clock.call(
        partial(attend_back_kernel, 128),
        [
            jax.ShapeDtypeStruct((6, length, D), jnp.bfloat16),
            jax.ShapeDtypeStruct((HEADS, length, length), jnp.bfloat16),
        ],
        [tokens, tokens, tokens_t, places, places, context_grad, attn_low, *probs],
        [first, second, value_pair, first, second, pair, pair] + prob_specs,
        [
            pl.BlockSpec((6, length, 2 * HD), lambda p: (0, 0, p)),
            pl.BlockSpec((2, length, length), lambda p: (p, 0, 0)),
        ],
        (HEADS // 2,),
        "attend_back",
        [
            pltpu.VMEM((length, length), jnp.float32),
            pltpu.VMEM((length, length), jnp.bfloat16),
        ],
    )


def bucket_kernel(group, one_ref, two_ref, *refs):
    grad_refs, (out_ref, sum_ref) = refs[:-2], refs[-2:]
    step = pl.program_id(0)
    rows, length = one_ref.shape
    buckets = NB1 + NB2

    @pl.when(step == 0)
    def clear():
        sum_ref[...] = jnp.zeros_like(sum_ref)

    first_ids = lax.broadcasted_iota(jnp.int32, (NB1, 1), 0)
    second_ids = lax.broadcasted_iota(jnp.int32, (NB2, 1), 0)
    hot, grads = [], []
    for start in range(0, rows, group):
        column = []
        for row in range(start, start + group):
            column.append(low((one_ref[row : row + 1, :] == first_ids).astype(jnp.float32)))
            column.append(low((two_ref[row : row + 1, :] == second_ids).astype(jnp.float32)))
        hot.append(jnp.concatenate(column, axis=0))
        parts = [ref[:, start : start + group, :].reshape(HEADS * group, length) for ref in grad_refs]
        grads.append(jnp.concatenate(parts, axis=0))
    sum_ref[...] += dot(jnp.concatenate(hot, axis=1), jnp.concatenate(grads, axis=1), 1, 1)

    @pl.when(step == pl.num_programs(0) - 1)
    def finish():
        member = lax.broadcasted_iota(jnp.int32, (1, sum_ref.shape[1]), 1) % group
        total = jnp.zeros((buckets, sum_ref.shape[1]), jnp.float32)
        for row in range(group):
            block = sum_ref[row * buckets : (row + 1) * buckets, :]
            total = total + jnp.where(member == row, block, 0.0)
        out_ref[...] = total


def bucket_sums(clock, rel_one, rel_two, score_grads):
    length = rel_one.shape[0]
    group, rows = 8, 32
    buckets = NB1 + NB2
    columns = len(score_grads) * HEADS * group
    rel = pl.BlockSpec((rows, length), lambda i: (i, 0))
    block = pl.BlockSpec((HEADS, rows, length), lambda i: (0, i, 0))
    sums = clock.call(
        partial(bucket_kernel, group),
        jax.ShapeDtypeStruct((buckets, columns), jnp.float32),
        [rel_one, rel_two, *score_grads],
        [rel, rel] + [block] * len(score_grads),
        whole_spec((buckets, columns)),
        (length // rows,),
        "bucket_sums",
        [pltpu.VMEM((group * buckets, columns), jnp.float32)],
    )
    sums = jnp.sum(sums.reshape(buckets, len(score_grads), HEADS, group), axis=3)
    return jnp.transpose(sums, (1, 2, 0))


def dp_strides(size):
    return tuple(1 << place for place in range(size.bit_length() - 1))


def orders(size):
    rest = dp_strides(size)[1:]
    if len(rest) < 2:
        return rest, rest
    return rest, (rest[1], rest[0]) + rest[2:]


def place(relative, order):
    spot = relative * 0
    for stride in order:
        spot = spot * 2 + (relative // (stride // 2)) % 2
    return spot


def rows_kernel(parts, order, ends, me_ref, *refs):
    left_refs, (right_ref, send_ref, keep_ref, sum_ref) = refs[:-4], refs[-4:]
    width = sum_ref.shape[0] // parts
    step = pl.program_id(0)
    right = right_ref[...].reshape(right_ref.shape[-2:])
    for index, left_ref in enumerate(left_refs):
        start = ends[index - 1] if index else 0

        @pl.when((step >= start) & (step < ends[index]))
        def product(left_ref=left_ref):
            sum_ref[...] = dot(left_ref[...], right, 0, 0)

    me = me_ref[0]
    core = me % 2
    for block in range(parts // 2):
        spot = place(jnp.bitwise_xor(block, me // 2), order)
        own = pl.ds(pl.multiple_of((2 * block + core) * width, 8), width)
        other = pl.ds(pl.multiple_of((2 * block + 1 - core) * width, 8), width)
        shape = (1,) * (len(keep_ref.shape) - 2) + (width, sum_ref.shape[1])
        keep_ref[pl.ds(spot, 1)] = sum_ref[own, :].reshape(shape)
        send_ref[pl.ds(spot, 1)] = sum_ref[other, :].reshape(shape)


def pair_kernel(me_ref, left_ref, right_ref, send_ref, keep_ref, sum_ref):
    width = sum_ref.shape[0] // 2
    sum_ref[...] = dot(left_ref[...], right_ref[...], 0, 0)
    core = me_ref[0] % 2
    own = pl.ds(pl.multiple_of(core * width, 8), width)
    other = pl.ds(pl.multiple_of((1 - core) * width, 8), width)
    keep_ref[0] = sum_ref[own, :]
    send_ref[0] = sum_ref[other, :]


def natural_blocks(values, me, size, order):
    blocks = values.reshape((size // 2, 2) + (values.shape[0] // size,) + values.shape[1:])
    spots = jnp.arange(size // 2, dtype=jnp.int32)
    relative = spots * 0
    for rank, stride in enumerate(reversed(order)):
        relative = relative + (spots >> rank) % 2 * (stride // 2)
    blocks = jnp.take(blocks, jnp.bitwise_xor(relative, me // 2), axis=0)
    core = me % 2
    own = lax.dynamic_index_in_dim(blocks, core, 1, keepdims=False)
    other = lax.dynamic_index_in_dim(blocks, 1 - core, 1, keepdims=False)
    return other, own


def wide_grad(clock, left, right, me, size, order):
    length, rows = left.shape
    wide = right.shape[1]
    width = rows // size
    if width % 8:
        return natural_blocks(dot(left, right, 0, 0), me[0], size, order)
    step = D
    half = size // 2
    block = pl.BlockSpec((half, width, step), lambda j, m: (0, 0, j))
    shape = jax.ShapeDtypeStruct((half, width, wide), jnp.float32)
    return clock.call(
        partial(rows_kernel, size, order, (wide // step,)),
        [shape, shape],
        [left, right],
        [whole_spec(left.shape), pl.BlockSpec((length, step), lambda j, m: (0, j))],
        [block, block],
        (wide // step,),
        "wide_grad",
        [pltpu.VMEM((rows, step), jnp.float32)],
        [me],
    )


def proj_grad(clock, lefts, right, first, me, size, order):
    length, rows = lefts[0][0].shape
    ends = []
    for left, count in lefts:
        ends.append(count + (ends[-1] if ends else 0))
    width = rows // size
    if width % 8:
        used = [left for left, count in lefts for at in range(count)]
        parts = jnp.stack([dot(left, right[first + j], 0, 0) for j, left in enumerate(used)])
        blocks = natural_blocks(jnp.swapaxes(parts, 0, 1), me[0], size, order)
        return [jnp.swapaxes(part, 1, 2) for part in blocks]
    half = size // 2
    block = pl.BlockSpec((half, 1, width, D), lambda j, m: (0, j, 0, 0))
    shape = jax.ShapeDtypeStruct((half, ends[-1], width, D), jnp.float32)
    return clock.call(
        partial(rows_kernel, size, order, tuple(ends)),
        [shape, shape],
        [left for left, count in lefts] + [right],
        [whole_spec((length, rows)) for left in lefts]
        + [pl.BlockSpec((1, length, D), lambda j, m: (first + j, 0, 0))],
        [block, block],
        (ends[-1],),
        "proj_grad",
        [pltpu.VMEM((rows, D), jnp.float32)],
        [me],
    )


def tall_grad(clock, left, right, me, size, order):
    length, rows = left.shape
    wide = right.shape[1]
    width = rows // size
    if width % 8 or 2 * width % LANES:
        return natural_blocks(dot(left, right, 0, 0), me[0], size, order)
    half = size // 2
    block = pl.BlockSpec(
        (1, width, wide), lambda i, m: (place(jnp.bitwise_xor(i, m[0] // 2), order), 0, 0)
    )
    shape = jax.ShapeDtypeStruct((half, width, wide), jnp.float32)
    return clock.call(
        pair_kernel,
        [shape, shape],
        [left, right],
        [pl.BlockSpec((length, 2 * width), lambda i, m: (0, i)), whole_spec(right.shape)],
        [block, block],
        (half,),
        "tall_grad",
        [pltpu.VMEM((2 * width, wide), jnp.float32)],
        [me],
    )


def swap_dp(values, stride, size):
    return lax.ppermute(values, "dp", [(index, index ^ stride) for index in range(size)])


def add_kernel(*refs):
    total = refs[0][...]
    for ref in refs[1:-1]:
        total = total + ref[...]
    refs[-1][...] = total


def add_blocks(clock, parts, first, count):
    shape = parts[0].shape[1:]
    tail = (0,) * len(shape)
    return clock.call(
        add_kernel,
        jax.ShapeDtypeStruct((count,) + shape, jnp.float32),
        parts,
        [pl.BlockSpec((1,) + shape, lambda i: (first + i,) + tail)] * len(parts),
        pl.BlockSpec((1,) + shape, lambda i: (i,) + tail),
        (count,),
        "add_blocks",
    )


class Reduction:
    def __init__(self, clock, blocks, order, size):
        self.clock = clock
        self.size = size
        self.order = list(order)
        send, keep = blocks
        self.parts = [keep, swap_dp(send, 1, size)]
        self.left = keep.shape[0]
        self.total = None

    def advance(self):
        if not self.order:
            self.total = add_blocks(self.clock, self.parts, 0, 1)[0]
            return
        self.left //= 2
        sent = add_blocks(self.clock, self.parts, self.left, self.left)
        self.parts.append(swap_dp(sent, self.order.pop(0), self.size))

    def finish(self):
        while self.total is None:
            self.advance()
        return self.total


def bins_kernel(half, at_ref, boxes_ref, grad_ref, send_ref, keep_ref):
    step = pl.program_id(0)
    width = keep_ref.shape[1]
    for ref, spot in ((keep_ref, step), (send_ref, step + half)):
        block = jnp.bitwise_xor(spot, at_ref[0])
        table = block // half
        ids = lax.broadcasted_iota(jnp.int32, (width, 1), 0) + (block - table * half) * width
        hot = low((boxes_ref[pl.ds(table, 1), :] == ids).astype(jnp.float32))
        ref[0] = dot(hot, grad_ref[...])


def table_grad(clock, boxes, grad, bins, at, parts):
    half = parts // 2
    width = 2 * bins // parts
    block = pl.BlockSpec((1, width, D), lambda i, m: (i, 0, 0))
    shape = jax.ShapeDtypeStruct((half, width, D), jnp.float32)
    return clock.call(
        partial(bins_kernel, half),
        [shape, shape],
        [boxes, grad],
        [whole_spec(boxes.shape), whole_spec(grad.shape)],
        [block, block],
        (half,),
        "table_grad",
        (),
        [at],
    )


def join_kernel(swapped, at_ref, *refs):
    parts, (out_ref, buffer, in_sem, out_sem) = refs[:-4], refs[-4:]
    arrive, leave = [], []
    spot = 0
    for part in parts:
        for block in range(part.shape[0]):
            to = jnp.bitwise_xor(spot, at_ref[0] & swapped)
            arrive.append(pltpu.make_async_copy(part.at[block], buffer.at[spot], in_sem.at[spot]))
            leave.append(pltpu.make_async_copy(buffer.at[spot], out_ref.at[to], out_sem.at[spot]))
            spot += 1
    for copy in arrive:
        copy.start()
    for first, second in zip(arrive, leave):
        first.wait()
        second.start()
    for copy in leave:
        copy.wait()


def join(clock, parts, at, swapped):
    count = sum(part.shape[0] for part in parts)
    shape = (count,) + parts[0].shape[1:]
    anywhere = pl.BlockSpec(memory_space=pl.ANY)
    return clock.call(
        partial(join_kernel, swapped),
        jax.ShapeDtypeStruct(shape, jnp.float32),
        parts,
        [anywhere] * len(parts),
        anywhere,
        (),
        "join",
        [
            pltpu.VMEM(shape, jnp.float32),
            pltpu.SemaphoreType.DMA((count,)),
            pltpu.SemaphoreType.DMA((count,)),
        ],
        [at],
    )


def halves_kernel(core_ref, own_ref, other_ref, out_ref):
    here = pl.program_id(0) == core_ref[0]

    @pl.when(here)
    def own():
        out_ref[0] = own_ref[...]

    @pl.when(jnp.logical_not(here))
    def other():
        out_ref[0] = other_ref[...]


def halves(clock, own, other, core):
    step = 4
    count = own.shape[0] // step
    block = (step,) + own.shape[1:]

    def spec(mine):
        def spot(half, i, c):
            here = (half == c[0]) if mine else (half != c[0])
            return (jnp.where(here, i, jnp.where(half == 0, 0, count - 1)), 0, 0)

        return pl.BlockSpec(block, spot)

    return clock.call(
        halves_kernel,
        jax.ShapeDtypeStruct((2,) + own.shape, jnp.float32),
        [own, other],
        [spec(True), spec(False)],
        pl.BlockSpec((1,) + block, lambda half, i, c: (half, i, 0, 0)),
        (2, count),
        "halves",
        (),
        [core],
    )


class EverySum:
    def __init__(self, clock, boxes, grad, bins, size):
        self.clock = clock
        self.size = size
        strides = dp_strides(size)
        self.steps = [strides[0], None] + list(strides[1:])
        dp_at = lax.axis_index("dp")
        at = dp_at * 0
        for stride in self.steps:
            bit = lax.axis_index("stream") if stride is None else dp_at // stride % 2
            at = at * 2 + bit
        self.at = at.astype(jnp.int32).reshape(1)
        send, keep = table_grad(clock, boxes, grad, bins, self.at, 2 * size)
        self.parts = [keep, self.swap(send, self.steps[0])]
        self.left = size
        self.down = self.steps[1:]
        self.up = list(reversed(self.steps))

    def swap(self, values, stride):
        if stride is None:
            return lax.ppermute(values, "stream", SWAP)
        return swap_dp(values, stride, self.size)

    def advance(self):
        if self.down:
            self.left //= 2
            sent = add_blocks(self.clock, self.parts, self.left, self.left)
            self.parts.append(self.swap(sent, self.down.pop(0)))
        elif self.up:
            if self.left:
                self.parts = [add_blocks(self.clock, self.parts, 0, 1)]
                self.left = 0
                sent = self.parts[0]
            else:
                swapped = self.size - 1 if len(self.up) == 1 else 0
                sent = join(self.clock, self.parts, self.at, swapped)
                self.parts = [sent]
            self.parts.append(self.swap(sent, self.up.pop(0)))

    def finish(self):
        while self.down or self.up:
            self.advance()
        return halves(self.clock, *self.parts, self.at // self.size)


class SmallSum:
    def __init__(self, clock, values, size):
        self.clock = clock
        self.size = size
        self.parts = [values[None]]
        self.strides = list(dp_strides(size))

    def advance(self):
        if len(self.parts) > 1:
            self.parts = [add_blocks(self.clock, self.parts, 0, 1)]
        if self.strides:
            self.parts.append(swap_dp(self.parts[0], self.strides.pop(0), self.size))

    def finish(self):
        while len(self.parts) > 1:
            self.advance()
        return self.parts[0][0]


def norm_back(grad, normal, root, gain):
    scaled = grad * gain
    inner = jnp.mean(scaled * normal, axis=-1, keepdims=True)
    outer = jnp.mean(scaled, axis=-1, keepdims=True)
    return (scaled - outer - normal * inner) * root


def norm_sums(grad, normal):
    return jnp.concatenate(
        [
            jnp.sum(grad * normal, axis=0, keepdims=True),
            jnp.sum(grad, axis=0, keepdims=True),
            jnp.zeros((6, grad.shape[1]), jnp.float32),
        ],
        axis=0,
    )


def second_kernel(grad_ref, normal_ref, root_ref, gain_ref, back_ref, low_ref, sums_ref):
    @pl.when(pl.program_id(0) == 0)
    def clear():
        sums_ref[...] = jnp.zeros_like(sums_ref)

    grad = grad_ref[...]
    back = norm_back(grad, normal_ref[...], root_ref[...], gain_ref[...])
    back_ref[...] = back
    low_ref[...] = low(back)
    sums_ref[...] += norm_sums(grad, normal_ref[...])


def second_back(clock, grad, normal, root, gain):
    length = grad.shape[0]
    step = 128
    rows = pl.BlockSpec((step, D), lambda i: (i, 0))
    return clock.call(
        second_kernel,
        [
            jax.ShapeDtypeStruct((length, D), jnp.float32),
            jax.ShapeDtypeStruct((length, D), jnp.bfloat16),
            jax.ShapeDtypeStruct((8, D), jnp.float32),
        ],
        [grad, normal, root, gain[None]],
        [rows, rows, pl.BlockSpec((step, 1), lambda i: (i, 0)), whole_spec((1, D))],
        [rows, rows, whole_spec((8, D))],
        (length // step,),
        "second_back",
    )


def inner_kernel(branch_ref, w_ref, inner_ref, out_ref):
    act_grad = dot(branch_ref[...], w_ref[...], 1, 1)
    inner = inner_ref[...]
    slope = 0.5 * (1.0 + lax.erf(inner * SQRT_HALF)) + inner * (
        DENSITY * jnp.exp(-0.5 * inner * inner)
    )
    out_ref[...] = low(act_grad * slope)


def inner_back(clock, branch_low, w_out, at, inner):
    length, wide = inner.shape
    step = 512
    cols = pl.BlockSpec((length, step), lambda j: (0, j))
    return clock.call(
        inner_kernel,
        jax.ShapeDtypeStruct((length, wide), jnp.bfloat16),
        [branch_low, w_out, inner],
        [
            whole_spec(branch_low.shape),
            pl.BlockSpec((None, None, step, D), lambda j: (0, at, j, 0)),
            cols,
        ],
        cols,
        (wide // step,),
        "inner_back",
    )


def first_kernel(
    inner_ref, w_ref, back_ref, normal_ref, root_ref, gain_ref, out_ref, sums_ref, sum_ref
):
    step = pl.program_id(0)
    part = dot(inner_ref[...], w_ref[...], 1, 1)

    @pl.when(step == 0)
    def start():
        sum_ref[...] = back_ref[...] + part

    @pl.when(step > 0)
    def more():
        sum_ref[...] += part

    @pl.when(step == pl.num_programs(0) - 1)
    def finish():
        tile = 128
        sums = jnp.zeros((8, D), jnp.float32)
        for at in range(0, sum_ref.shape[0], tile):
            span = slice(at, at + tile)
            grad = sum_ref[span, :]
            out_ref[span, :] = norm_back(
                grad, normal_ref[span, :], root_ref[span, :], gain_ref[...]
            )
            sums = sums + norm_sums(grad, normal_ref[span, :])
        sums_ref[...] = sums


def first_back(clock, inner_low, w_in, at, sum_grad, normal, root, gain):
    length, wide = inner_low.shape
    step = 768
    return clock.call(
        first_kernel,
        [
            jax.ShapeDtypeStruct((length, D), jnp.float32),
            jax.ShapeDtypeStruct((8, D), jnp.float32),
        ],
        [inner_low, w_in, sum_grad, normal, root, gain[None]],
        [
            pl.BlockSpec((length, step), lambda j: (0, j)),
            pl.BlockSpec((None, None, D, step), lambda j: (0, at, 0, j)),
            whole_spec((length, D)),
            whole_spec((length, D)),
            whole_spec((length, 1)),
            whole_spec((1, D)),
        ],
        [whole_spec((length, D)), whole_spec((8, D))],
        (wide // step,),
        "first_back",
        [pltpu.VMEM((length, D), jnp.float32)],
    )


def context_kernel(count_ref, own_ref, other_ref, w_ref, out_ref, attn_ref):
    rows = own_ref.shape[0]
    mask = (lax.broadcasted_iota(jnp.int32, (rows, 1), 0) < count_ref[0]).astype(jnp.float32)
    attn = low((own_ref[...] + other_ref[...]) * mask)
    attn_ref[...] = attn
    out_ref[...] = low(dot(attn, w_ref[...], 1, 1))


def context_back(clock, count, own, other, out_w, at):
    shape = jax.ShapeDtypeStruct(own.shape, jnp.bfloat16)
    return clock.call(
        context_kernel,
        [shape, shape],
        [own, other, out_w],
        [
            whole_spec(own.shape),
            whole_spec(own.shape),
            pl.BlockSpec((None, None, D, D), lambda i, c: (0, at, 0, 0)),
        ],
        [whole_spec(own.shape), whole_spec(own.shape)],
        (1,),
        "context_back",
        (),
        [count],
    )


def input_kernel(grad_ref, w_ref, start_ref, out_ref):
    step = pl.program_id(0)
    part = dot(grad_ref[0], w_ref[0], 1, 1)

    @pl.when(step == 0)
    def start():
        out_ref[...] = start_ref[...] + part

    @pl.when(step > 0)
    def more():
        out_ref[...] += part


def input_back(clock, grads, weights, at, start, first, count):
    length = grads.shape[1]
    return clock.call(
        input_kernel,
        jax.ShapeDtypeStruct(start.shape, jnp.float32),
        [grads, weights, start],
        [
            pl.BlockSpec((1, length, D), lambda j: (first + j, 0, 0)),
            pl.BlockSpec((None, None, 1, D, D), lambda j: (0, at, first + j, 0, 0)),
            whole_spec(start.shape),
        ],
        whole_spec(start.shape),
        (count,),
        "input_back",
    )


def normalize(values):
    center = values - jnp.mean(values, axis=-1, keepdims=True)
    root = lax.rsqrt(jnp.mean(center * center, axis=-1, keepdims=True) + EPS)
    return center * root, root


def swap_stream(values):
    return lax.ppermute(values, "stream", SWAP)


def local(
    dp_size,
    tokens,
    boxes,
    rel_one,
    rel_two,
    vis_count,
    spatial_tables,
    proj_weights,
    out_weights,
    ffn_in,
    ffn_out,
    norm_gains,
    norm_shifts,
    bias_tables,
    cotangent,
):
    length = tokens.shape[2]
    stream_at = lax.axis_index("stream")
    me = lax.axis_index("dp").astype(jnp.int32).reshape(1)
    count = jnp.where(stream_at == 0, length, vis_count).astype(jnp.int32)
    rowmask = (jnp.arange(length, dtype=jnp.int32)[:, None] < count[0]).astype(jnp.float32)
    rel = (rel_one[0, 0], rel_two[0, 0])
    bin_ids = jnp.arange(spatial_tables.shape[1], dtype=jnp.int32)
    hot_x = low(boxes[0, 0, 0][:, None] == bin_ids[None, :])
    hot_y = low(boxes[0, 0, 1][:, None] == bin_ids[None, :])
    spatial = low(dot(hot_x, spatial_tables[0]) + dot(hot_y, spatial_tables[1]))
    tables = bias_tables[0].astype(jnp.float32)
    tables = jnp.stack(
        [
            jnp.pad(tables[:, :, :NB1], ((0, 0), (0, 0), (0, LANES - NB1))),
            jnp.pad(tables[:, :, NB1:], ((0, 0), (0, 0), (0, LANES - NB2))),
        ],
        axis=1,
    )

    clock = Order()
    chunks = 2
    rows = length // chunks
    hidden = rounded = tokens[0, 0]
    kept = []
    places = project(clock, spatial, proj_weights, 0, 3, 2, 1)
    biases = [None] * chunks
    for layer_at in range(LAYERS):
        last = layer_at + 1 == LAYERS
        projected = (*project(clock, rounded, proj_weights, layer_at, 0, 3, 1), *places)
        context, states, probs, moved, next_biases = (), (), [], [], []
        for at in range(chunks):
            bias = biases[at]
            if bias is None:
                bias = score_bias(clock, *rel, tables[layer_at], at, rows)
            context, attn, prob = attend(
                clock, count, projected, bias, out_weights, layer_at, at, rows, context
            )
            context = (context,)
            probs.append(prob)
            moved.append((attn, swap_stream(attn)))
        for at in range(chunks):
            states = feed_forward(
                clock,
                hidden,
                *moved[at],
                norm_gains[0, layer_at],
                norm_shifts[0, layer_at],
                ffn_in,
                ffn_out,
                layer_at,
                at,
                states,
            )
            if not last and at + 1 < chunks:
                for part in range(chunks):
                    next_biases.append(score_bias(clock, *rel, tables[layer_at + 1], part, rows))
                places = project(clock, spatial, proj_weights, layer_at + 1, 3, 2, 1)
        biases = next_biases
        result, result_low, first, first_root, normed_low, inner, activated, second, second_root = states
        kept.append(
            (
                rounded,
                projected,
                context[0],
                probs,
                (first, first_root),
                normed_low,
                inner,
                activated,
                (second, second_root),
            )
        )
        hidden, rounded = result, result_low
    output = low(hidden * rowmask)[None, None]

    grad = cotangent[0, 0].astype(jnp.float32) * rowmask
    both_orders = orders(dp_size)
    step_order = {
        name + layer: both_orders[name + layer in NEAR]
        for name in ("tall", "wide", "token", "place")
        for layer in "01"
    }
    moves = {}
    state = {"grad1": grad}

    def move(name, blocks):
        moves[name] = Reduction(clock, blocks, step_order[name], dp_size)

    def second(layer):
        gains = norm_gains[0, int(layer)]
        normal, root = kept[int(layer)][8]
        results = second_back(clock, state["grad" + layer], normal, root, gains[1])
        state["sum" + layer], state["branch" + layer], state["second_sums" + layer] = results

    def tall(layer):
        activated = kept[int(layer)][7]
        name = "tall" + layer
        move(name, tall_grad(clock, activated, state["branch" + layer], me, dp_size, step_order[name]))

    def inner(layer):
        state["inner" + layer] = inner_back(
            clock, state["branch" + layer], ffn_out, int(layer), kept[int(layer)][6]
        )

    def wide(layer):
        normed_low = kept[int(layer)][5]
        name = "wide" + layer
        move(name, wide_grad(clock, normed_low, state["inner" + layer], me, dp_size, step_order[name]))

    def first(layer):
        normal, root = kept[int(layer)][4]
        gains = norm_gains[0, int(layer)]
        state["first" + layer], state["first_sums" + layer] = first_back(
            clock,
            state["inner" + layer],
            ffn_in,
            int(layer),
            state["sum" + layer],
            normal,
            root,
            gains[0],
        )
        state["other" + layer] = swap_stream(state["first" + layer])

    def context(layer):
        state["context" + layer], state["attn" + layer] = context_back(
            clock, count, state["first" + layer], state["other" + layer], out_weights, int(layer)
        )

    def attention(layer):
        state["proj" + layer], state["scores" + layer] = attend_back(
            clock,
            kept[int(layer)][1],
            kept[int(layer)][3],
            state["context" + layer],
            state["attn" + layer],
        )

    def token(layer):
        lefts = [(kept[int(layer)][0], 3)]
        name = "token" + layer
        move(name, proj_grad(clock, lefts, state["proj" + layer], 0, me, dp_size, step_order[name]))

    def place_step(layer):
        lefts = [(spatial, 2), (kept[int(layer)][2], 1)]
        name = "place" + layer
        move(name, proj_grad(clock, lefts, state["proj" + layer], 3, me, dp_size, step_order[name]))

    def dx(layer):
        grad = input_back(
            clock, state["proj" + layer], proj_weights, int(layer), state["first" + layer], 0, 3
        )
        state["grad" + str(int(layer) - 1)] = grad

    def space(layer):
        last = int(layer) + 1 == LAYERS
        start = jnp.zeros((length, D), jnp.float32) if last else state["space" + str(int(layer) + 1)]
        state["space" + layer] = input_back(
            clock, state["proj" + layer], proj_weights, int(layer), start, 3, 2
        )

    bins = spatial_tables.shape[1]

    def table(layer):
        moves["all0"] = EverySum(clock, boxes[0, 0], low(state["space0"]), bins, dp_size)

    def bucket(layer):
        scores = [state["scores" + at] for at in "01"]
        state["buckets"] = bucket_sums(clock, rel[0], rel[1], scores)

    def tiny(layer):
        norms = []
        for at in "01":
            sums = (state["first_sums" + at], state["second_sums" + at])
            norms += [sums[0][0], sums[1][0], sums[0][1], sums[1][1]]
        parts = (jnp.stack(norms), state["buckets"])
        flat = jnp.concatenate([part.reshape(-1, LANES) for part in parts], axis=0)
        moves["norms0"] = SmallSum(clock, flat, dp_size)

    kernels = (
        second,
        tall,
        inner,
        wide,
        first,
        context,
        attention,
        token,
        place_step,
        dx,
        space,
        table,
        bucket,
        tiny,
    )
    for step in PLAN:
        name, layer = step // 2, str(step % 2)
        if name < len(kernels):
            kernels[name](layer)
        else:
            moves[NAMES[name - len(kernels)] + layer].advance()
    owns = {name: moves[name].finish() for name in step_order}
    layers = "01"
    scattered = (
        jnp.stack([jnp.concatenate([owns["token" + at], owns["place" + at][:2]]) for at in layers]),
        jnp.stack([owns["place" + at][2] for at in layers]),
        jnp.stack([owns["wide" + at] for at in layers]),
        jnp.stack([owns["tall" + at] for at in layers]),
    )
    shared = moves["all0"].finish().reshape(2, bins, D)
    flat = moves["norms0"].finish()
    normed = flat[: 4 * LAYERS * D // LANES].reshape(LAYERS, 4, D)
    width = D // dp_size
    normed = lax.dynamic_slice_in_dim(normed, me[0] * width, width, 2)
    bucket_own = flat[4 * LAYERS * D // LANES :].reshape(1, LAYERS, HEADS, NB1 + NB2)
    return (
        output,
        state["grad-1"][None, None],
        shared,
        *(part[None] for part in scattered),
        normed[None, :, :2],
        normed[None, :, 2:],
        bucket_own,
    )


NAMES = ("tall", "wide", "token", "place", "all", "norms")
(SECOND0, SECOND1, TALL0, TALL1, INNER0, INNER1, WIDE0, WIDE1, FIRST0, FIRST1) = range(10)
(CONTEXT0, CONTEXT1, ATTEND0, ATTEND1, TOKEN0, TOKEN1, PLACE0, PLACE1, DX0, DX1) = range(10, 20)
(SPACE0, SPACE1, TABLE0, TABLE1, BUCKET0, BUCKET1, TINY0, TINY1) = range(20, 28)
(T0, T1, W0, W1, K0, K1, P0, P1, A0, A1, N0, N1) = range(28, 40)
NEAR = ("wide1", "place1", "wide0",)
PLAN = (
    SECOND1, TALL1, INNER1, WIDE1, FIRST1, T1, W1, CONTEXT1, ATTEND1, T1, DX1, PLACE1, W1, TOKEN1,
    T1, P1, SECOND0, K1, TALL0, W1, T1, INNER0, SPACE1, WIDE0, W1, FIRST0, K1, T0, W0, P1, CONTEXT0,
    ATTEND0, SPACE0, TABLE0, P1, K1, A0, W0, T0, K1, W0, A0, PLACE0, P1, TOKEN0, P0, A0, K0, T0, A0,
    BUCKET0, W0, A0, TINY0, A0, P0, A0, DX0, K0, A0, P0, N0, N0, T0, N0, K0, A0, K0, N0, P0, A0,
)


def solution(mesh):
    placed = (
        P("stream", "dp", None, None),
        P("stream", "dp", None, None),
        P("stream", "dp", None, None),
        P("stream", "dp", None, None),
        P("dp"),
        P(),
        P("stream", None, None, None, None),
        P("stream", None, None, None),
        P("stream", None, None, None),
        P("stream", None, None, None),
        P("stream", None, None, None),
        P("stream", None, None, None),
        P("stream", None, None, None),
        P("stream", "dp", None, None),
    )
    return jax.shard_map(
        partial(local, mesh.shape["dp"]),
        mesh=mesh,
        in_specs=placed,
        out_specs=(
            P("stream", "dp", None, None),
            P("stream", "dp", None, None),
            P(),
            P("stream", None, None, "dp", None),
            P("stream", None, "dp", None),
            P("stream", None, "dp", None),
            P("stream", None, "dp", None),
            P("stream", None, None, "dp"),
            P("stream", None, None, "dp"),
            P("stream", None, None, None),
        ),
        check_vma=False,
    )
```

```python
from functools import partial

import jax
import jax.numpy as jnp
from jax import lax
from jax.experimental import pallas as pl
from jax.experimental.pallas import tpu as pltpu
from jax.sharding import PartitionSpec as P

D = 768
HEADS = 12
HD = 64
NB1 = 32
NB2 = 64
LAYERS = 2
LANES = 128
NEG_FILL = -1e30
EPS = 1e-05
SCALE = HD ** (-0.5)
SQRT_HALF = 0.5**0.5
DENSITY = 0.3989422804014327
SWAP = [(0, 1), (1, 0)]
VMEM_LIMIT = 48 << 20
COST = pl.CostEstimate(flops=10**13, bytes_accessed=10**9, transcendentals=0)


def dot(left, right, left_dim=1, right_dim=0):
    return lax.dot_general(
        left, right, (((left_dim,), (right_dim,)), ((), ())), preferred_element_type=jnp.float32
    )


def low(values):
    return values.astype(jnp.bfloat16)


def gate(values, *deps):
    return lax.optimization_barrier((values,) + deps)[0]


class Order:
    def __init__(self):
        self.last = ()

    def call(
        self,
        kernel,
        shapes,
        operands,
        in_specs,
        out_specs,
        grid,
        name,
        scratch=(),
        scalars=(),
        carried=(),
        mark=0,
    ):
        after = tuple(self.last)
        if any(one is other for one in after for other in carried):
            after = ()
        taken = len(scalars) + len(operands)
        unread = len(carried) + len(after)

        def body(*refs):
            kernel(*refs[:taken], *refs[taken + unread :])

        single = not isinstance(shapes, list)
        results = pl.pallas_call(
            body,
            grid_spec=pltpu.PrefetchScalarGridSpec(
                num_scalar_prefetch=len(scalars),
                grid=grid,
                in_specs=list(in_specs) + [pl.BlockSpec(memory_space=pl.ANY)] * unread,
                out_specs=out_specs,
                scratch_shapes=list(scratch),
            ),
            out_shape=shapes,
            input_output_aliases={taken + at: at for at in range(len(carried))},
            compiler_params=pltpu.CompilerParams(vmem_limit_bytes=VMEM_LIMIT),
            cost_estimate=COST,
            name=name,
        )(*scalars, *operands, *carried, *after)
        self.last = (results if single else results[mark],)
        return results


def whole_spec(shape):
    return pl.BlockSpec(shape, lambda *ids: (0,) * len(shape))


def bias_kernel(one_ref, two_ref, table_ref, bias_ref):
    rows, length = one_ref.shape

    def group(step, carry):
        span = pl.ds(pl.multiple_of(step * 8, 8), 8)
        for col in range(0, length, LANES):
            cols = slice(col, col + LANES)
            first = one_ref[span, cols]
            second = two_ref[span, cols]
            for head in range(HEADS):
                first_row = jnp.broadcast_to(table_ref[0, head : head + 1, :], (8, LANES))
                second_row = jnp.broadcast_to(table_ref[1, head : head + 1, :], (8, LANES))
                bias_ref[head, span, cols] = jnp.take_along_axis(
                    first_row, first, axis=1
                ) + jnp.take_along_axis(second_row, second, axis=1)
        return carry

    lax.fori_loop(0, rows // 8, group, 0)


def score_bias(clock, rel_one, rel_two, table, at, rows):
    length = rel_one.shape[1]
    step = 64
    first = at * rows // step
    rel = pl.BlockSpec((step, length), lambda i: (first + i, 0))
    return clock.call(
        bias_kernel,
        jax.ShapeDtypeStruct((HEADS, rows, length), jnp.float32),
        [rel_one, rel_two, table],
        [rel, rel, whole_spec(table.shape)],
        pl.BlockSpec((HEADS, step, length), lambda i: (0, i, 0)),
        (rows // step,),
        "score_bias",
    )


def attend_kernel(
    at,
    tile,
    count_ref,
    query_ref,
    key_ref,
    value_ref,
    squery_ref,
    skey_ref,
    bias_ref,
    out_w_ref,
    context_ref,
    attn_ref,
    prob_ref,
    score_ref,
    low_ref,
):
    pair = pl.program_id(0)
    rows = query_ref.shape[0]
    length = value_ref.shape[0]
    lanes = lax.broadcasted_iota(jnp.int32, (1, 2 * HD), 1)
    valid = lax.broadcasted_iota(jnp.int32, (1, length), 1) < count_ref[0]
    keys = jnp.concatenate([key_ref[...], skey_ref[...]], axis=0)
    for half in range(2):
        keep = low(((lanes >= HD) == (half == 1)).astype(jnp.float32) * SCALE)
        queries = jnp.concatenate([query_ref[...] * keep, squery_ref[...] * keep], axis=1)
        score_ref[half] = dot(queries, keys)

    def group(step, carry):
        span = pl.ds(pl.multiple_of(step * tile, tile), tile)
        for half in range(2):
            scores = score_ref[half, span, :] + bias_ref[half, span, :]
            scores = jnp.where(valid, scores, NEG_FILL)
            weights = jnp.exp(scores - jnp.max(scores, axis=1, keepdims=True))
            prob = weights * (1.0 / jnp.sum(weights, axis=1, keepdims=True))
            prob_ref[half, span, :] = prob
            low_ref[half, span, :] = low(prob)
        return carry

    lax.fori_loop(0, rows // tile, group, 0)
    first = dot(low_ref[0], value_ref[...])
    second = dot(low_ref[1], value_ref[...])
    cols = pl.ds(pl.multiple_of(pair * 2 * HD, 2 * HD), 2 * HD)
    context_ref[:, cols] = low(jnp.where(lanes >= HD, second, first))

    @pl.when(pair == pl.num_programs(0) - 1)
    def finish():
        index = lax.broadcasted_iota(jnp.int32, (rows, 1), 0) + at * rows
        mask = (index < count_ref[0]).astype(jnp.float32)
        attn_ref[...] = dot(context_ref[...], out_w_ref[...]) * mask


def project_kernel(flipped, left_ref, w_ref, out_ref, flip_ref):
    step = pl.program_id(0)
    result = low(dot(left_ref[...], w_ref[...]))
    out_ref[...] = result

    @pl.when(step >= flipped)
    def flip():
        flip_ref[...] = result.T


def project(clock, left, weights, layer_at, first, count, flipped):
    length = left.shape[0]
    return clock.call(
        partial(project_kernel, flipped),
        [
            jax.ShapeDtypeStruct((count, length, D), jnp.bfloat16),
            jax.ShapeDtypeStruct((count - flipped, D, length), jnp.bfloat16),
        ],
        [left, weights],
        [
            whole_spec((length, D)),
            pl.BlockSpec((None, None, None, D, D), lambda j: (0, layer_at, first + j, 0, 0)),
        ],
        [
            pl.BlockSpec((None, length, D), lambda j: (j, 0, 0)),
            pl.BlockSpec((None, D, length), lambda j: (jnp.maximum(j - flipped, 0), 0, 0)),
        ],
        (count,),
        "project",
    )


def attend(clock, count, projected, bias, out_w, layer_at, at, rows, carried):
    tokens, tokens_t, places, places_t = projected
    length = tokens.shape[1]
    row_pair = pl.BlockSpec((None, rows, 2 * HD), lambda p, c: (0, at, p))
    key_pair = pl.BlockSpec((None, 2 * HD, length), lambda p, c: (0, p, 0))
    value_pair = pl.BlockSpec((None, length, 2 * HD), lambda p, c: (2, 0, p))
    score_pair = pl.BlockSpec((2, rows, length), lambda p, c: (p, 0, 0))
    return clock.call(
        partial(attend_kernel, at, 128),
        [
            jax.ShapeDtypeStruct((length, D), jnp.bfloat16),
            jax.ShapeDtypeStruct((rows, D), jnp.float32),
            jax.ShapeDtypeStruct((HEADS, rows, length), jnp.float32),
        ],
        [tokens, tokens_t, tokens, places, places_t, bias, out_w],
        [
            row_pair,
            key_pair,
            value_pair,
            row_pair,
            key_pair,
            score_pair,
            pl.BlockSpec((None, None, D, D), lambda p, c: (0, layer_at, 0, 0)),
        ],
        [pl.BlockSpec((rows, D), lambda p, c: (at, 0)), whole_spec((rows, D)), score_pair],
        (HEADS // 2,),
        "attend",
        [
            pltpu.VMEM((2, rows, length), jnp.float32),
            pltpu.VMEM((2, rows, length), jnp.bfloat16),
        ],
        [count],
        carried,
        1,
    )


def ffn_kernel(
    x_ref,
    own_ref,
    other_ref,
    gain_ref,
    shift_ref,
    w_in_ref,
    w_out_ref,
    result_ref,
    rounded_ref,
    first_ref,
    first_root_ref,
    low_ref,
    inner_ref,
    act_ref,
    second_ref,
    second_root_ref,
    sum_ref,
):
    step = pl.program_id(0)

    @pl.when(step == 0)
    def start():
        normal, root = normalize(
            x_ref[...].astype(jnp.float32) + (own_ref[...] + other_ref[...])
        )
        normed = normal * gain_ref[0:1, :] + shift_ref[0:1, :]
        first_ref[...] = normal
        first_root_ref[...] = root
        low_ref[...] = low(normed)
        sum_ref[...] = normed

    inner = dot(low_ref[...], w_in_ref[...])
    inner_ref[...] = inner
    act = low(0.5 * inner * (1.0 + lax.erf(inner * SQRT_HALF)))
    act_ref[...] = act
    sum_ref[...] += dot(act, w_out_ref[...])

    @pl.when(step == pl.num_programs(0) - 1)
    def finish():
        normal, root = normalize(sum_ref[...])
        second_ref[...] = normal
        second_root_ref[...] = root
        result = normal * gain_ref[1:2, :] + shift_ref[1:2, :]
        result_ref[...] = result
        rounded_ref[...] = low(result)


def feed_forward(clock, x, own, other, gains, shifts, w_in, w_out, layer_at, at, carried):
    length = x.shape[0]
    rows = own.shape[0]
    wide = w_in.shape[-1]
    step = D
    narrow = pl.BlockSpec((rows, D), lambda j: (at, 0))
    thin = pl.BlockSpec((rows, 1), lambda j: (at, 0))
    broad = pl.BlockSpec((rows, step), lambda j: (at, j))

    def shape(columns, kind):
        return jax.ShapeDtypeStruct((length, columns), kind)

    return clock.call(
        ffn_kernel,
        [
            shape(D, jnp.float32),
            shape(D, jnp.bfloat16),
            shape(D, jnp.float32),
            shape(1, jnp.float32),
            shape(D, jnp.bfloat16),
            shape(wide, jnp.float32),
            shape(wide, jnp.bfloat16),
            shape(D, jnp.float32),
            shape(1, jnp.float32),
        ],
        [x, own, other, gains, shifts, w_in, w_out],
        [
            narrow,
            whole_spec((rows, D)),
            whole_spec((rows, D)),
            whole_spec((2, D)),
            whole_spec((2, D)),
            pl.BlockSpec((None, None, D, step), lambda j: (0, layer_at, 0, j)),
            pl.BlockSpec((None, None, step, D), lambda j: (0, layer_at, j, 0)),
        ],
        [narrow, narrow, narrow, thin, narrow, broad, broad, narrow, thin],
        (wide // step,),
        "feed_forward",
        [pltpu.VMEM((rows, D), jnp.float32)],
        (),
        carried,
    )


def attend_back_kernel(
    tile,
    *refs,
):
    (query_ref, key_ref, value_ref, squery_ref, skey_ref, grad_ref), refs = refs[:6], refs[6:]
    attn_ref, refs = refs[0], refs[1:]
    prob_refs, (out_ref, score_out_ref, dprob_ref, prob_low_ref) = refs[:-4], refs[-4:]
    rows = prob_refs[0].shape[1]
    lanes = lax.broadcasted_iota(jnp.int32, (1, 2 * HD), 1)
    queries = jnp.concatenate([query_ref[...], squery_ref[...]], axis=1)
    keys = jnp.concatenate([key_ref[...], skey_ref[...]], axis=1)
    grads = grad_ref[...]
    results = []
    for half in range(2):
        own = low(((lanes >= HD) == (half == 1)).astype(jnp.float32))
        dprob_ref[...] = dot(grads * own, value_ref[...])
        for chunk, prob_ref in enumerate(prob_refs):

            def group(step, carry, chunk=chunk, prob_ref=prob_ref):
                span = pl.ds(pl.multiple_of(step * tile, tile), tile)
                there = pl.ds(pl.multiple_of(chunk * rows + step * tile, tile), tile)
                prob = prob_ref[half, span, :]
                dprob = dprob_ref[there, :]
                total = jnp.sum(prob * dprob, axis=1, keepdims=True)
                score_out_ref[half, there, :] = low(prob * (dprob - total))
                prob_low_ref[there, :] = low(prob)
                return carry

            lax.fori_loop(0, rows // tile, group, 0)
        scores = score_out_ref[half]
        results.append(
            (
                dot(scores, keys) * SCALE,
                dot(scores, queries, 0, 0) * SCALE,
                dot(prob_low_ref[...], grads, 0, 0),
            )
        )
    (dq0, dk0, dv0), (dq1, dk1, dv1) = results
    upper = lanes >= HD
    wide = 2 * HD
    out_ref[0] = low(jnp.where(upper, dq1[:, :wide], dq0[:, :wide]))
    out_ref[1] = low(jnp.where(upper, dk1[:, :wide], dk0[:, :wide]))
    out_ref[2] = low(jnp.where(upper, dv1, dv0))
    out_ref[3] = low(jnp.where(upper, dq1[:, wide:], dq0[:, wide:]))
    out_ref[4] = low(jnp.where(upper, dk1[:, wide:], dk0[:, wide:]))
    out_ref[5] = attn_ref[...]


def attend_back(clock, projected, probs, context_grad, attn_low):
    tokens, tokens_t, places, places_t = projected
    length = tokens.shape[1]
    pair = pl.BlockSpec((length, 2 * HD), lambda p: (0, p))
    first = pl.BlockSpec((None, length, 2 * HD), lambda p: (0, 0, p))
    second = pl.BlockSpec((None, length, 2 * HD), lambda p: (1, 0, p))
    value_pair = pl.BlockSpec((None, 2 * HD, length), lambda p: (1, p, 0))
    prob_specs = [pl.BlockSpec((2,) + prob.shape[1:], lambda p: (p, 0, 0)) for prob in probs]
    return clock.call(
        partial(attend_back_kernel, 128),
        [
            jax.ShapeDtypeStruct((6, length, D), jnp.bfloat16),
            jax.ShapeDtypeStruct((HEADS, length, length), jnp.bfloat16),
        ],
        [tokens, tokens, tokens_t, places, places, context_grad, attn_low, *probs],
        [first, second, value_pair, first, second, pair, pair] + prob_specs,
        [
            pl.BlockSpec((6, length, 2 * HD), lambda p: (0, 0, p)),
            pl.BlockSpec((2, length, length), lambda p: (p, 0, 0)),
        ],
        (HEADS // 2,),
        "attend_back",
        [
            pltpu.VMEM((length, length), jnp.float32),
            pltpu.VMEM((length, length), jnp.bfloat16),
        ],
    )


def bucket_kernel(group, one_ref, two_ref, *refs):
    grad_refs, (out_ref, sum_ref) = refs[:-2], refs[-2:]
    step = pl.program_id(0)
    rows, length = one_ref.shape
    buckets = NB1 + NB2

    @pl.when(step == 0)
    def clear():
        sum_ref[...] = jnp.zeros_like(sum_ref)

    first_ids = lax.broadcasted_iota(jnp.int32, (NB1, 1), 0)
    second_ids = lax.broadcasted_iota(jnp.int32, (NB2, 1), 0)
    hot, grads = [], []
    for start in range(0, rows, group):
        column = []
        for row in range(start, start + group):
            column.append(low((one_ref[row : row + 1, :] == first_ids).astype(jnp.float32)))
            column.append(low((two_ref[row : row + 1, :] == second_ids).astype(jnp.float32)))
        hot.append(jnp.concatenate(column, axis=0))
        parts = [ref[:, start : start + group, :].reshape(HEADS * group, length) for ref in grad_refs]
        grads.append(jnp.concatenate(parts, axis=0))
    sum_ref[...] += dot(jnp.concatenate(hot, axis=1), jnp.concatenate(grads, axis=1), 1, 1)

    @pl.when(step == pl.num_programs(0) - 1)
    def finish():
        member = lax.broadcasted_iota(jnp.int32, (1, sum_ref.shape[1]), 1) % group
        total = jnp.zeros((buckets, sum_ref.shape[1]), jnp.float32)
        for row in range(group):
            block = sum_ref[row * buckets : (row + 1) * buckets, :]
            total = total + jnp.where(member == row, block, 0.0)
        out_ref[...] = total


def bucket_sums(clock, rel_one, rel_two, score_grads):
    length = rel_one.shape[0]
    group, rows = 8, 32
    buckets = NB1 + NB2
    columns = len(score_grads) * HEADS * group
    rel = pl.BlockSpec((rows, length), lambda i: (i, 0))
    block = pl.BlockSpec((HEADS, rows, length), lambda i: (0, i, 0))
    sums = clock.call(
        partial(bucket_kernel, group),
        jax.ShapeDtypeStruct((buckets, columns), jnp.float32),
        [rel_one, rel_two, *score_grads],
        [rel, rel] + [block] * len(score_grads),
        whole_spec((buckets, columns)),
        (length // rows,),
        "bucket_sums",
        [pltpu.VMEM((group * buckets, columns), jnp.float32)],
    )
    sums = jnp.sum(sums.reshape(buckets, len(score_grads), HEADS, group), axis=3)
    return jnp.transpose(sums, (1, 2, 0))


def dp_strides(size):
    return tuple(1 << place for place in range(size.bit_length() - 1))


def orders(size):
    rest = dp_strides(size)[1:]
    if len(rest) < 2:
        return rest, rest
    return rest, (rest[1], rest[0]) + rest[2:]


def place(relative, order):
    spot = relative * 0
    for stride in order:
        spot = spot * 2 + (relative // (stride // 2)) % 2
    return spot


def rows_kernel(parts, order, ends, me_ref, *refs):
    left_refs, (right_ref, send_ref, keep_ref, sum_ref) = refs[:-4], refs[-4:]
    width = sum_ref.shape[0] // parts
    step = pl.program_id(0)
    right = right_ref[...].reshape(right_ref.shape[-2:])
    for index, left_ref in enumerate(left_refs):
        start = ends[index - 1] if index else 0

        @pl.when((step >= start) & (step < ends[index]))
        def product(left_ref=left_ref):
            sum_ref[...] = dot(left_ref[...], right, 0, 0)

    me = me_ref[0]
    core = me % 2
    for block in range(parts // 2):
        spot = place(jnp.bitwise_xor(block, me // 2), order)
        own = pl.ds(pl.multiple_of((2 * block + core) * width, 8), width)
        other = pl.ds(pl.multiple_of((2 * block + 1 - core) * width, 8), width)
        shape = (1,) * (len(keep_ref.shape) - 2) + (width, sum_ref.shape[1])
        keep_ref[pl.ds(spot, 1)] = sum_ref[own, :].reshape(shape)
        send_ref[pl.ds(spot, 1)] = sum_ref[other, :].reshape(shape)


def pair_kernel(me_ref, left_ref, right_ref, send_ref, keep_ref, sum_ref):
    width = sum_ref.shape[0] // 2
    sum_ref[...] = dot(left_ref[...], right_ref[...], 0, 0)
    core = me_ref[0] % 2
    own = pl.ds(pl.multiple_of(core * width, 8), width)
    other = pl.ds(pl.multiple_of((1 - core) * width, 8), width)
    keep_ref[0] = sum_ref[own, :]
    send_ref[0] = sum_ref[other, :]


def natural_blocks(values, me, size, order):
    blocks = values.reshape((size // 2, 2) + (values.shape[0] // size,) + values.shape[1:])
    spots = jnp.arange(size // 2, dtype=jnp.int32)
    relative = spots * 0
    for rank, stride in enumerate(reversed(order)):
        relative = relative + (spots >> rank) % 2 * (stride // 2)
    blocks = jnp.take(blocks, jnp.bitwise_xor(relative, me // 2), axis=0)
    core = me % 2
    own = lax.dynamic_index_in_dim(blocks, core, 1, keepdims=False)
    other = lax.dynamic_index_in_dim(blocks, 1 - core, 1, keepdims=False)
    return other, own


def wide_grad(clock, left, right, me, size, order):
    length, rows = left.shape
    wide = right.shape[1]
    width = rows // size
    if width % 8:
        return natural_blocks(dot(left, right, 0, 0), me[0], size, order)
    step = D
    half = size // 2
    block = pl.BlockSpec((half, width, step), lambda j, m: (0, 0, j))
    shape = jax.ShapeDtypeStruct((half, width, wide), jnp.float32)
    return clock.call(
        partial(rows_kernel, size, order, (wide // step,)),
        [shape, shape],
        [left, right],
        [whole_spec(left.shape), pl.BlockSpec((length, step), lambda j, m: (0, j))],
        [block, block],
        (wide // step,),
        "wide_grad",
        [pltpu.VMEM((rows, step), jnp.float32)],
        [me],
    )


def proj_grad(clock, lefts, right, first, me, size, order):
    length, rows = lefts[0][0].shape
    ends = []
    for left, count in lefts:
        ends.append(count + (ends[-1] if ends else 0))
    width = rows // size
    if width % 8:
        used = [left for left, count in lefts for at in range(count)]
        parts = jnp.stack([dot(left, right[first + j], 0, 0) for j, left in enumerate(used)])
        blocks = natural_blocks(jnp.swapaxes(parts, 0, 1), me[0], size, order)
        return [jnp.swapaxes(part, 1, 2) for part in blocks]
    half = size // 2
    block = pl.BlockSpec((half, 1, width, D), lambda j, m: (0, j, 0, 0))
    shape = jax.ShapeDtypeStruct((half, ends[-1], width, D), jnp.float32)
    return clock.call(
        partial(rows_kernel, size, order, tuple(ends)),
        [shape, shape],
        [left for left, count in lefts] + [right],
        [whole_spec((length, rows)) for left in lefts]
        + [pl.BlockSpec((1, length, D), lambda j, m: (first + j, 0, 0))],
        [block, block],
        (ends[-1],),
        "proj_grad",
        [pltpu.VMEM((rows, D), jnp.float32)],
        [me],
    )


def tall_grad(clock, left, right, me, size, order):
    length, rows = left.shape
    wide = right.shape[1]
    width = rows // size
    if width % 8 or 2 * width % LANES:
        return natural_blocks(dot(left, right, 0, 0), me[0], size, order)
    half = size // 2
    block = pl.BlockSpec(
        (1, width, wide), lambda i, m: (place(jnp.bitwise_xor(i, m[0] // 2), order), 0, 0)
    )
    shape = jax.ShapeDtypeStruct((half, width, wide), jnp.float32)
    return clock.call(
        pair_kernel,
        [shape, shape],
        [left, right],
        [pl.BlockSpec((length, 2 * width), lambda i, m: (0, i)), whole_spec(right.shape)],
        [block, block],
        (half,),
        "tall_grad",
        [pltpu.VMEM((2 * width, wide), jnp.float32)],
        [me],
    )


def swap_dp(values, stride, size):
    return lax.ppermute(values, "dp", [(index, index ^ stride) for index in range(size)])


def add_kernel(*refs):
    total = refs[0][...]
    for ref in refs[1:-1]:
        total = total + ref[...]
    refs[-1][...] = total


def add_blocks(clock, parts, first, count):
    shape = parts[0].shape[1:]
    tail = (0,) * len(shape)
    return clock.call(
        add_kernel,
        jax.ShapeDtypeStruct((count,) + shape, jnp.float32),
        parts,
        [pl.BlockSpec((1,) + shape, lambda i: (first + i,) + tail)] * len(parts),
        pl.BlockSpec((1,) + shape, lambda i: (i,) + tail),
        (count,),
        "add_blocks",
    )


class Reduction:
    def __init__(self, clock, blocks, order, size):
        self.clock = clock
        self.size = size
        self.order = list(order)
        send, keep = blocks
        self.parts = [keep, swap_dp(send, 1, size)]
        self.left = keep.shape[0]
        self.total = None

    def advance(self):
        if not self.order:
            self.total = add_blocks(self.clock, self.parts, 0, 1)[0]
            return
        self.left //= 2
        sent = add_blocks(self.clock, self.parts, self.left, self.left)
        self.parts.append(swap_dp(sent, self.order.pop(0), self.size))

    def finish(self):
        while self.total is None:
            self.advance()
        return self.total


def bins_kernel(half, at_ref, boxes_ref, grad_ref, send_ref, keep_ref):
    step = pl.program_id(0)
    width = keep_ref.shape[1]
    for ref, spot in ((keep_ref, step), (send_ref, step + half)):
        block = jnp.bitwise_xor(spot, at_ref[0])
        table = block // half
        ids = lax.broadcasted_iota(jnp.int32, (width, 1), 0) + (block - table * half) * width
        hot = low((boxes_ref[pl.ds(table, 1), :] == ids).astype(jnp.float32))
        ref[0] = dot(hot, grad_ref[...])


def table_grad(clock, boxes, grad, bins, at, parts):
    half = parts // 2
    width = 2 * bins // parts
    block = pl.BlockSpec((1, width, D), lambda i, m: (i, 0, 0))
    shape = jax.ShapeDtypeStruct((half, width, D), jnp.float32)
    return clock.call(
        partial(bins_kernel, half),
        [shape, shape],
        [boxes, grad],
        [whole_spec(boxes.shape), whole_spec(grad.shape)],
        [block, block],
        (half,),
        "table_grad",
        (),
        [at],
    )


def join_kernel(swapped, at_ref, *refs):
    parts, (out_ref, buffer, in_sem, out_sem) = refs[:-4], refs[-4:]
    arrive, leave = [], []
    spot = 0
    for part in parts:
        for block in range(part.shape[0]):
            to = jnp.bitwise_xor(spot, at_ref[0] & swapped)
            arrive.append(pltpu.make_async_copy(part.at[block], buffer.at[spot], in_sem.at[spot]))
            leave.append(pltpu.make_async_copy(buffer.at[spot], out_ref.at[to], out_sem.at[spot]))
            spot += 1
    for copy in arrive:
        copy.start()
    for first, second in zip(arrive, leave):
        first.wait()
        second.start()
    for copy in leave:
        copy.wait()


def join(clock, parts, at, swapped):
    count = sum(part.shape[0] for part in parts)
    shape = (count,) + parts[0].shape[1:]
    anywhere = pl.BlockSpec(memory_space=pl.ANY)
    return clock.call(
        partial(join_kernel, swapped),
        jax.ShapeDtypeStruct(shape, jnp.float32),
        parts,
        [anywhere] * len(parts),
        anywhere,
        (),
        "join",
        [
            pltpu.VMEM(shape, jnp.float32),
            pltpu.SemaphoreType.DMA((count,)),
            pltpu.SemaphoreType.DMA((count,)),
        ],
        [at],
    )


def halves_kernel(core_ref, own_ref, other_ref, out_ref):
    here = pl.program_id(0) == core_ref[0]

    @pl.when(here)
    def own():
        out_ref[0] = own_ref[...]

    @pl.when(jnp.logical_not(here))
    def other():
        out_ref[0] = other_ref[...]


def halves(clock, own, other, core):
    step = 4
    count = own.shape[0] // step
    block = (step,) + own.shape[1:]

    def spec(mine):
        def spot(half, i, c):
            here = (half == c[0]) if mine else (half != c[0])
            return (jnp.where(here, i, jnp.where(half == 0, 0, count - 1)), 0, 0)

        return pl.BlockSpec(block, spot)

    return clock.call(
        halves_kernel,
        jax.ShapeDtypeStruct((2,) + own.shape, jnp.float32),
        [own, other],
        [spec(True), spec(False)],
        pl.BlockSpec((1,) + block, lambda half, i, c: (half, i, 0, 0)),
        (2, count),
        "halves",
        (),
        [core],
    )


class EverySum:
    def __init__(self, clock, boxes, grad, bins, size):
        self.clock = clock
        self.size = size
        strides = dp_strides(size)
        self.steps = [strides[0], None] + list(strides[1:])
        dp_at = lax.axis_index("dp")
        at = dp_at * 0
        for stride in self.steps:
            bit = lax.axis_index("stream") if stride is None else dp_at // stride % 2
            at = at * 2 + bit
        self.at = at.astype(jnp.int32).reshape(1)
        send, keep = table_grad(clock, boxes, grad, bins, self.at, 2 * size)
        self.parts = [keep, self.swap(send, self.steps[0])]
        self.left = size
        self.down = self.steps[1:]
        self.up = list(reversed(self.steps))

    def swap(self, values, stride):
        if stride is None:
            return lax.ppermute(values, "stream", SWAP)
        return swap_dp(values, stride, self.size)

    def advance(self):
        if self.down:
            self.left //= 2
            sent = add_blocks(self.clock, self.parts, self.left, self.left)
            self.parts.append(self.swap(sent, self.down.pop(0)))
        elif self.up:
            if self.left:
                self.parts = [add_blocks(self.clock, self.parts, 0, 1)]
                self.left = 0
                sent = self.parts[0]
            else:
                swapped = self.size - 1 if len(self.up) == 1 else 0
                sent = join(self.clock, self.parts, self.at, swapped)
                self.parts = [sent]
            self.parts.append(self.swap(sent, self.up.pop(0)))

    def finish(self):
        while self.down or self.up:
            self.advance()
        return halves(self.clock, *self.parts, self.at // self.size)


class SmallSum:
    def __init__(self, clock, values, size):
        self.clock = clock
        self.size = size
        self.parts = [values[None]]
        self.strides = list(dp_strides(size))

    def advance(self):
        if len(self.parts) > 1:
            self.parts = [add_blocks(self.clock, self.parts, 0, 1)]
        if self.strides:
            self.parts.append(swap_dp(self.parts[0], self.strides.pop(0), self.size))

    def finish(self):
        while len(self.parts) > 1:
            self.advance()
        return self.parts[0][0]


def norm_back(grad, normal, root, gain):
    scaled = grad * gain
    inner = jnp.mean(scaled * normal, axis=-1, keepdims=True)
    outer = jnp.mean(scaled, axis=-1, keepdims=True)
    return (scaled - outer - normal * inner) * root


def norm_sums(grad, normal):
    return jnp.concatenate(
        [
            jnp.sum(grad * normal, axis=0, keepdims=True),
            jnp.sum(grad, axis=0, keepdims=True),
            jnp.zeros((6, grad.shape[1]), jnp.float32),
        ],
        axis=0,
    )


def second_kernel(grad_ref, normal_ref, root_ref, gain_ref, back_ref, low_ref, sums_ref):
    @pl.when(pl.program_id(0) == 0)
    def clear():
        sums_ref[...] = jnp.zeros_like(sums_ref)

    grad = grad_ref[...]
    back = norm_back(grad, normal_ref[...], root_ref[...], gain_ref[...])
    back_ref[...] = back
    low_ref[...] = low(back)
    sums_ref[...] += norm_sums(grad, normal_ref[...])


def second_back(clock, grad, normal, root, gain):
    length = grad.shape[0]
    step = 128
    rows = pl.BlockSpec((step, D), lambda i: (i, 0))
    return clock.call(
        second_kernel,
        [
            jax.ShapeDtypeStruct((length, D), jnp.float32),
            jax.ShapeDtypeStruct((length, D), jnp.bfloat16),
            jax.ShapeDtypeStruct((8, D), jnp.float32),
        ],
        [grad, normal, root, gain[None]],
        [rows, rows, pl.BlockSpec((step, 1), lambda i: (i, 0)), whole_spec((1, D))],
        [rows, rows, whole_spec((8, D))],
        (length // step,),
        "second_back",
    )


def inner_kernel(branch_ref, w_ref, inner_ref, out_ref):
    act_grad = dot(branch_ref[...], w_ref[...], 1, 1)
    inner = inner_ref[...]
    slope = 0.5 * (1.0 + lax.erf(inner * SQRT_HALF)) + inner * (
        DENSITY * jnp.exp(-0.5 * inner * inner)
    )
    out_ref[...] = low(act_grad * slope)


def inner_back(clock, branch_low, w_out, at, inner):
    length, wide = inner.shape
    step = 512
    cols = pl.BlockSpec((length, step), lambda j: (0, j))
    return clock.call(
        inner_kernel,
        jax.ShapeDtypeStruct((length, wide), jnp.bfloat16),
        [branch_low, w_out, inner],
        [
            whole_spec(branch_low.shape),
            pl.BlockSpec((None, None, step, D), lambda j: (0, at, j, 0)),
            cols,
        ],
        cols,
        (wide // step,),
        "inner_back",
    )


def first_kernel(
    inner_ref, w_ref, back_ref, normal_ref, root_ref, gain_ref, out_ref, sums_ref, sum_ref
):
    step = pl.program_id(0)
    part = dot(inner_ref[...], w_ref[...], 1, 1)

    @pl.when(step == 0)
    def start():
        sum_ref[...] = back_ref[...] + part

    @pl.when(step > 0)
    def more():
        sum_ref[...] += part

    @pl.when(step == pl.num_programs(0) - 1)
    def finish():
        tile = 128
        sums = jnp.zeros((8, D), jnp.float32)
        for at in range(0, sum_ref.shape[0], tile):
            span = slice(at, at + tile)
            grad = sum_ref[span, :]
            out_ref[span, :] = norm_back(
                grad, normal_ref[span, :], root_ref[span, :], gain_ref[...]
            )
            sums = sums + norm_sums(grad, normal_ref[span, :])
        sums_ref[...] = sums


def first_back(clock, inner_low, w_in, at, sum_grad, normal, root, gain):
    length, wide = inner_low.shape
    step = 768
    return clock.call(
        first_kernel,
        [
            jax.ShapeDtypeStruct((length, D), jnp.float32),
            jax.ShapeDtypeStruct((8, D), jnp.float32),
        ],
        [inner_low, w_in, sum_grad, normal, root, gain[None]],
        [
            pl.BlockSpec((length, step), lambda j: (0, j)),
            pl.BlockSpec((None, None, D, step), lambda j: (0, at, 0, j)),
            whole_spec((length, D)),
            whole_spec((length, D)),
            whole_spec((length, 1)),
            whole_spec((1, D)),
        ],
        [whole_spec((length, D)), whole_spec((8, D))],
        (wide // step,),
        "first_back",
        [pltpu.VMEM((length, D), jnp.float32)],
    )


def context_kernel(count_ref, own_ref, other_ref, w_ref, out_ref, attn_ref):
    rows = own_ref.shape[0]
    mask = (lax.broadcasted_iota(jnp.int32, (rows, 1), 0) < count_ref[0]).astype(jnp.float32)
    attn = low((own_ref[...] + other_ref[...]) * mask)
    attn_ref[...] = attn
    out_ref[...] = low(dot(attn, w_ref[...], 1, 1))


def context_back(clock, count, own, other, out_w, at):
    shape = jax.ShapeDtypeStruct(own.shape, jnp.bfloat16)
    return clock.call(
        context_kernel,
        [shape, shape],
        [own, other, out_w],
        [
            whole_spec(own.shape),
            whole_spec(own.shape),
            pl.BlockSpec((None, None, D, D), lambda i, c: (0, at, 0, 0)),
        ],
        [whole_spec(own.shape), whole_spec(own.shape)],
        (1,),
        "context_back",
        (),
        [count],
    )


def input_kernel(grad_ref, w_ref, start_ref, out_ref):
    step = pl.program_id(0)
    part = dot(grad_ref[0], w_ref[0], 1, 1)

    @pl.when(step == 0)
    def start():
        out_ref[...] = start_ref[...] + part

    @pl.when(step > 0)
    def more():
        out_ref[...] += part


def input_back(clock, grads, weights, at, start, first, count):
    length = grads.shape[1]
    return clock.call(
        input_kernel,
        jax.ShapeDtypeStruct(start.shape, jnp.float32),
        [grads, weights, start],
        [
            pl.BlockSpec((1, length, D), lambda j: (first + j, 0, 0)),
            pl.BlockSpec((None, None, 1, D, D), lambda j: (0, at, first + j, 0, 0)),
            whole_spec(start.shape),
        ],
        whole_spec(start.shape),
        (count,),
        "input_back",
    )


def normalize(values):
    center = values - jnp.mean(values, axis=-1, keepdims=True)
    root = lax.rsqrt(jnp.mean(center * center, axis=-1, keepdims=True) + EPS)
    return center * root, root


def swap_stream(values):
    return lax.ppermute(values, "stream", SWAP)


def local(
    dp_size,
    tokens,
    boxes,
    rel_one,
    rel_two,
    vis_count,
    spatial_tables,
    proj_weights,
    out_weights,
    ffn_in,
    ffn_out,
    norm_gains,
    norm_shifts,
    bias_tables,
    cotangent,
):
    length = tokens.shape[2]
    stream_at = lax.axis_index("stream")
    me = lax.axis_index("dp").astype(jnp.int32).reshape(1)
    count = jnp.where(stream_at == 0, length, vis_count).astype(jnp.int32)
    rowmask = (jnp.arange(length, dtype=jnp.int32)[:, None] < count[0]).astype(jnp.float32)
    rel = (rel_one[0, 0], rel_two[0, 0])
    bin_ids = jnp.arange(spatial_tables.shape[1], dtype=jnp.int32)
    hot_x = low(boxes[0, 0, 0][:, None] == bin_ids[None, :])
    hot_y = low(boxes[0, 0, 1][:, None] == bin_ids[None, :])
    spatial = low(dot(hot_x, spatial_tables[0]) + dot(hot_y, spatial_tables[1]))
    tables = bias_tables[0].astype(jnp.float32)
    tables = jnp.stack(
        [
            jnp.pad(tables[:, :, :NB1], ((0, 0), (0, 0), (0, LANES - NB1))),
            jnp.pad(tables[:, :, NB1:], ((0, 0), (0, 0), (0, LANES - NB2))),
        ],
        axis=1,
    )

    clock = Order()
    chunks = 2
    rows = length // chunks
    hidden = rounded = tokens[0, 0]
    kept = []
    places = project(clock, spatial, proj_weights, 0, 3, 2, 1)
    biases = [None] * chunks
    for layer_at in range(LAYERS):
        last = layer_at + 1 == LAYERS
        projected = (*project(clock, rounded, proj_weights, layer_at, 0, 3, 1), *places)
        context, states, probs, moved, next_biases = (), (), [], [], []
        for at in range(chunks):
            bias = biases[at]
            if bias is None:
                bias = score_bias(clock, *rel, tables[layer_at], at, rows)
            context, attn, prob = attend(
                clock, count, projected, bias, out_weights, layer_at, at, rows, context
            )
            context = (context,)
            probs.append(prob)
            moved.append((attn, swap_stream(attn)))
        for at in range(chunks):
            states = feed_forward(
                clock,
                hidden,
                *moved[at],
                norm_gains[0, layer_at],
                norm_shifts[0, layer_at],
                ffn_in,
                ffn_out,
                layer_at,
                at,
                states,
            )
            if not last and at + 1 < chunks:
                for part in range(chunks):
                    next_biases.append(score_bias(clock, *rel, tables[layer_at + 1], part, rows))
                places = project(clock, spatial, proj_weights, layer_at + 1, 3, 2, 1)
        biases = next_biases
        result, result_low, first, first_root, normed_low, inner, activated, second, second_root = states
        kept.append(
            (
                rounded,
                projected,
                context[0],
                probs,
                (first, first_root),
                normed_low,
                inner,
                activated,
                (second, second_root),
            )
        )
        hidden, rounded = result, result_low
    output = low(hidden * rowmask)[None, None]

    grad = cotangent[0, 0].astype(jnp.float32) * rowmask
    both_orders = orders(dp_size)
    step_order = {
        name + layer: both_orders[name + layer in NEAR]
        for name in ("tall", "wide", "token", "place")
        for layer in "01"
    }
    moves = {}
    state = {"grad1": grad}

    def move(name, blocks):
        moves[name] = Reduction(clock, blocks, step_order[name], dp_size)

    def second(layer):
        gains = norm_gains[0, int(layer)]
        normal, root = kept[int(layer)][8]
        results = second_back(clock, state["grad" + layer], normal, root, gains[1])
        state["sum" + layer], state["branch" + layer], state["second_sums" + layer] = results

    def tall(layer):
        activated = kept[int(layer)][7]
        name = "tall" + layer
        move(name, tall_grad(clock, activated, state["branch" + layer], me, dp_size, step_order[name]))

    def inner(layer):
        state["inner" + layer] = inner_back(
            clock, state["branch" + layer], ffn_out, int(layer), kept[int(layer)][6]
        )

    def wide(layer):
        normed_low = kept[int(layer)][5]
        name = "wide" + layer
        move(name, wide_grad(clock, normed_low, state["inner" + layer], me, dp_size, step_order[name]))

    def first(layer):
        normal, root = kept[int(layer)][4]
        gains = norm_gains[0, int(layer)]
        state["first" + layer], state["first_sums" + layer] = first_back(
            clock,
            state["inner" + layer],
            ffn_in,
            int(layer),
            state["sum" + layer],
            normal,
            root,
            gains[0],
        )
        state["other" + layer] = swap_stream(state["first" + layer])

    def context(layer):
        state["context" + layer], state["attn" + layer] = context_back(
            clock, count, state["first" + layer], state["other" + layer], out_weights, int(layer)
        )

    def attention(layer):
        state["proj" + layer], state["scores" + layer] = attend_back(
            clock,
            kept[int(layer)][1],
            kept[int(layer)][3],
            state["context" + layer],
            state["attn" + layer],
        )

    def token(layer):
        lefts = [(kept[int(layer)][0], 3)]
        name = "token" + layer
        move(name, proj_grad(clock, lefts, state["proj" + layer], 0, me, dp_size, step_order[name]))

    def place_step(layer):
        lefts = [(spatial, 2), (kept[int(layer)][2], 1)]
        name = "place" + layer
        move(name, proj_grad(clock, lefts, state["proj" + layer], 3, me, dp_size, step_order[name]))

    def dx(layer):
        grad = input_back(
            clock, state["proj" + layer], proj_weights, int(layer), state["first" + layer], 0, 3
        )
        state["grad" + str(int(layer) - 1)] = grad

    def space(layer):
        last = int(layer) + 1 == LAYERS
        start = jnp.zeros((length, D), jnp.float32) if last else state["space" + str(int(layer) + 1)]
        state["space" + layer] = input_back(
            clock, state["proj" + layer], proj_weights, int(layer), start, 3, 2
        )

    bins = spatial_tables.shape[1]

    def table(layer):
        moves["all0"] = EverySum(clock, boxes[0, 0], low(state["space0"]), bins, dp_size)

    def bucket(layer):
        scores = [state["scores" + at] for at in "01"]
        state["buckets"] = bucket_sums(clock, rel[0], rel[1], scores)

    def tiny(layer):
        norms = []
        for at in "01":
            sums = (state["first_sums" + at], state["second_sums" + at])
            norms += [sums[0][0], sums[1][0], sums[0][1], sums[1][1]]
        parts = (jnp.stack(norms), state["buckets"])
        flat = jnp.concatenate([part.reshape(-1, LANES) for part in parts], axis=0)
        moves["norms0"] = SmallSum(clock, flat, dp_size)

    kernels = (
        second,
        tall,
        inner,
        wide,
        first,
        context,
        attention,
        token,
        place_step,
        dx,
        space,
        table,
        bucket,
        tiny,
    )
    for step in PLAN:
        name, layer = step // 2, str(step % 2)
        if name < len(kernels):
            kernels[name](layer)
        else:
            moves[NAMES[name - len(kernels)] + layer].advance()
    owns = {name: moves[name].finish() for name in step_order}
    layers = "01"
    scattered = (
        jnp.stack([jnp.concatenate([owns["token" + at], owns["place" + at][:2]]) for at in layers]),
        jnp.stack([owns["place" + at][2] for at in layers]),
        jnp.stack([owns["wide" + at] for at in layers]),
        jnp.stack([owns["tall" + at] for at in layers]),
    )
    shared = moves["all0"].finish().reshape(2, bins, D)
    flat = moves["norms0"].finish()
    normed = flat[: 4 * LAYERS * D // LANES].reshape(LAYERS, 4, D)
    width = D // dp_size
    normed = lax.dynamic_slice_in_dim(normed, me[0] * width, width, 2)
    bucket_own = flat[4 * LAYERS * D // LANES :].reshape(1, LAYERS, HEADS, NB1 + NB2)
    return (
        output,
        state["grad-1"][None, None],
        shared,
        *(part[None] for part in scattered),
        normed[None, :, :2],
        normed[None, :, 2:],
        bucket_own,
    )


NAMES = ("tall", "wide", "token", "place", "all", "norms")
(SECOND0, SECOND1, TALL0, TALL1, INNER0, INNER1, WIDE0, WIDE1, FIRST0, FIRST1) = range(10)
(CONTEXT0, CONTEXT1, ATTEND0, ATTEND1, TOKEN0, TOKEN1, PLACE0, PLACE1, DX0, DX1) = range(10, 20)
(SPACE0, SPACE1, TABLE0, TABLE1, BUCKET0, BUCKET1, TINY0, TINY1) = range(20, 28)
(T0, T1, W0, W1, K0, K1, P0, P1, A0, A1, N0, N1) = range(28, 40)
NEAR = ("wide1", "place1", "wide0",)
PLAN = (
    SECOND1, TALL1, INNER1, WIDE1, FIRST1, T1, W1, CONTEXT1, ATTEND1, T1, PLACE1, W1, DX1, TOKEN1,
    T1, P1, K1, SECOND0, TALL0, W1, INNER0, T1, SPACE1, WIDE0, W1, FIRST0, K1, W0, T0, P1, CONTEXT0,
    ATTEND0, SPACE0, TABLE0, K1, P1, A0, W0, T0, K1, W0, A0, PLACE0, TOKEN0, P0, A0, K0, T0, P1, A0,
    BUCKET0, W0, DX0, A0, TINY0, A0, P0, A0, K0, A0, N0, P0, T0, N0, N0, K0, N0, A0, K0, P0, A0,
)


def solution(mesh):
    placed = (
        P("stream", "dp", None, None),
        P("stream", "dp", None, None),
        P("stream", "dp", None, None),
        P("stream", "dp", None, None),
        P("dp"),
        P(),
        P("stream", None, None, None, None),
        P("stream", None, None, None),
        P("stream", None, None, None),
        P("stream", None, None, None),
        P("stream", None, None, None),
        P("stream", None, None, None),
        P("stream", None, None, None),
        P("stream", "dp", None, None),
    )
    return jax.shard_map(
        partial(local, mesh.shape["dp"]),
        mesh=mesh,
        in_specs=placed,
        out_specs=(
            P("stream", "dp", None, None),
            P("stream", "dp", None, None),
            P(),
            P("stream", None, None, "dp", None),
            P("stream", None, "dp", None),
            P("stream", None, "dp", None),
            P("stream", None, "dp", None),
            P("stream", None, None, "dp"),
            P("stream", None, None, "dp"),
            P("stream", None, None, None),
        ),
        check_vma=False,
    )
```
